32 devices in a mesh: seq: 4 (over x, core), mp: 8 (over z, y).
Axes of the slice: x: 2, y: 2, z: 4, core: 2. Of those that a mesh axis runs over, the one named last changes fastest.
Arguments:
- signal: bfloat16 [2048, 8192], P('seq', 'mp'), may hold values from -6 to 6
- gate_input: bfloat16 [2048, 8192], P('seq', 'mp'), may hold values from -6 to 6
- input_map: bfloat16 [2048, 128], P('seq'), may hold values from -0.5 to 0.5
- output_map: bfloat16 [2048, 128], P('seq'), may hold values from -6 to 6
- log_decay: float32 [2048, 128], P('seq', 'mp'), may hold values from -1 to 0
- step_size: float32 [2048, 128], P('seq', 'mp'), may hold values from 0.003 to 0.03
- skip_gain: float32 [128], P('mp'), may hold values from 0.1 to 1.9
- norm_gain: float32 [8192], P('mp'), may hold values from 0.1 to 1.9
- out_weight: bfloat16 [8192, 8192], P('mp'), may hold values from -0.09375 to 0.09375
Outputs:
- mixed_out: bfloat16 [2048, 8192], P('seq', 'mp')
The draws below stay inside these ranges and needn't reach their ends.
All inputs are finite; a program needn't handle non-finite values.
Results may differ from the reference program's by a relative error of at most 0.024.
Values may be sent and summed in bfloat16 or wider, within the bound.
A program may use at most 64 MiB of HBM per device.

```python
import math
import jax
import jax.numpy as jnp
from jax import lax

D = 8192
HEADS = 128
HEAD_DIM = 64
STATE = 128
BLOCK = 256
TOK_DEV = 512
INNER = 8192
TOKEN_COUNT = 2048
N_MP = 8


def draw_log_decay(key, part):
    subkeys = jax.random.split(key, 7)
    fast_share = 0.4
    fast_heads = jax.random.uniform(subkeys[0], (HEADS,)) < fast_share
    fast_rates = jnp.exp(jax.random.uniform(subkeys[1], (HEADS,), minval=math.log(1.0 / 50.0), maxval=math.log(1.0 / 30.0)))
    slow_rates = jnp.exp(jax.random.uniform(subkeys[2], (HEADS,), minval=math.log(0.02), maxval=math.log(0.25))) * 2.3 / TOKEN_COUNT
    baseline_rates = jnp.where(fast_heads, fast_rates, slow_rates)
    surface_rough = jnp.exp(jax.random.uniform(subkeys[3], (TOKEN_COUNT, HEADS), minval=-math.log(2.0), maxval=math.log(2.0)))
    processor_factor = jnp.exp(jax.random.uniform(subkeys[4], (TOKEN_COUNT // TOK_DEV, 1), minval=-math.log(2.0), maxval=math.log(2.0)))
    processor_factor = jnp.repeat(processor_factor, TOK_DEV, axis=0)
    token_positions = jax.random.randint(subkeys[5], (2,), 0, TOKEN_COUNT)
    spike_row_set = jnp.any(jnp.arange(TOKEN_COUNT)[:, None] == token_positions[None, :], axis=1)
    loss_values = jnp.log(jax.random.uniform(subkeys[6], (TOKEN_COUNT, HEADS), minval=0.5, maxval=0.8))
    value_entries = -(baseline_rates[None, :] * surface_rough * processor_factor) + jnp.where(spike_row_set[:, None], loss_values, 0.0)
    return value_entries.astype(jnp.float32)


def raised(values, key, source, target, shards_of, factor):
    owner, partner = [(jnp.arange(values.shape[dim]) // (values.shape[dim] // shards_of)).reshape([-1 if axis == dim else 1 for axis in range(values.ndim)]) for dim in (source, target)]
    chosen = jax.random.permutation(key, shards_of)[partner]
    strong = (owner == chosen) | (owner == (partner + shards_of // 2) % shards_of)
    return jnp.where(strong, factor * values, values)


def steps_of(key, dims, cuts, low, top_value):
    def one(position, blocks):
        heights = jax.random.uniform(jax.random.fold_in(jax.random.fold_in(key, 6), position), (blocks,), jnp.float32, low / len(cuts), top_value / len(cuts))
        return jnp.repeat(jnp.exp(heights), dims[position] // blocks).reshape((-1,) + (1,) * (len(dims) - position - 1))

    level = one(*cuts[0])
    for cut in cuts[1:]:
        level = level * one(*cut)
    return level


def gaussian(own_key, shape, spread, reach, cuts=(), held_as=jnp.bfloat16):
    values = jax.random.normal(own_key, shape, jnp.float32) * spread
    if len(cuts) > 0:
        values = steps_of(own_key, shape, cuts, -0.22, 0.18) * values
    return jnp.clip(values, min=-reach, max=reach).astype(held_as)


def noise_with(own_key, extent, scale, most, shards, heavy, dtype=jnp.bfloat16):
    drawn = scale * jax.random.normal(own_key, extent, jnp.float32)
    if shards:
        drawn = drawn * steps_of(own_key, extent, shards, -0.22, 0.18)
    return jnp.clip(raised(drawn, jax.random.fold_in(own_key, 3), *heavy), -most, most).astype(dtype)


def setup_inputs(seed: int = 0) -> dict:
    streams_of = jax.random.split(jax.random.key(seed), 10)
    signal = gaussian(streams_of[0], (TOKEN_COUNT, INNER), 1.0, 6.0, ((0, 4), (1, 8)))
    gate_input = gaussian(streams_of[1], (TOKEN_COUNT, INNER), 1.0, 6.0, ((0, 4), (1, 8)))
    input_map = gaussian(streams_of[2], (TOKEN_COUNT, STATE), STATE ** -0.5, 0.5, ((0, 4),))
    output_map = gaussian(streams_of[3], (TOKEN_COUNT, STATE), 1.0, 6.0, ((0, 4),))
    log_decay = draw_log_decay(jax.random.fold_in(streams_of[9], 71), 0)
    step_size = jnp.clip(jnp.exp(math.log(0.03) - 2.3025851 * jax.random.uniform(streams_of[5], (TOKEN_COUNT, HEADS), jnp.float32) ** steps_of(streams_of[5], (TOKEN_COUNT, HEADS), ((0, 4), (1, 8)), -0.2, 0.2)), 0.003, 0.03)
    skip_gain = jnp.clip(1.0 + 0.18 * jax.random.normal(streams_of[6], (HEADS,), jnp.float32), 0.1, 1.9)
    norm_gain = jnp.clip(1.0 + 0.18 * jax.random.normal(streams_of[7], (INNER,), jnp.float32), 0.1, 1.9)
    out_weight = noise_with(streams_of[8], (INNER, D), INNER ** -0.5, 0.09375, ((0, 8),), (0, 1, 8, 2.0))
    return dict(signal=signal, gate_input=gate_input, input_map=input_map, output_map=output_map, log_decay=log_decay, step_size=step_size, skip_gain=skip_gain, norm_gain=norm_gain, out_weight=out_weight)


def block_terms(pieces):
    signal_blk, keys_blk, query_blk, decay_blk, steps_blk = pieces
    cumulative = jnp.cumsum(decay_blk, axis=0)
    scores = jnp.dot(query_blk, keys_blk.T, preferred_element_type=jnp.float32)
    log_gaps = cumulative[:, None, :] - cumulative[None, :, :]
    causal = jnp.arange(BLOCK)[:, None] >= jnp.arange(BLOCK)[None, :]
    decays = jnp.exp(jnp.where(causal[:, :, None], log_gaps, -jnp.inf))
    weights = (scores[:, :, None] * decays * steps_blk[None, :, :]).astype(jnp.bfloat16)
    inner_part = jnp.einsum('tsh,shp->thp', weights.astype(jnp.float32), signal_blk.astype(jnp.float32))
    feed_rows = (signal_blk.astype(jnp.float32) * (steps_blk * jnp.exp(cumulative[-1] - cumulative))[:, :, None]).astype(jnp.bfloat16)
    local_state = jnp.einsum('shp,sn->hpn', feed_rows.astype(jnp.float32), keys_blk.astype(jnp.float32))
    return (inner_part, local_state, cumulative)

def reference(signal, gate_input, input_map, output_map, log_decay, step_size, skip_gain, norm_gain, out_weight):
    block_count = TOKEN_COUNT // BLOCK
    signal_blk = signal.reshape(block_count, BLOCK, HEADS, HEAD_DIM)
    keys_blk = input_map.reshape(block_count, BLOCK, STATE)
    query_blk = output_map.reshape(block_count, BLOCK, STATE)
    decay_blk = log_decay.reshape(block_count, BLOCK, HEADS)
    steps_blk = step_size.reshape(block_count, BLOCK, HEADS)
    inner_part, local_state, cumulative = lax.map(block_terms, (signal_blk, keys_blk, query_blk, decay_blk, steps_blk))
    block_total = cumulative[:, -1, :]

    def advance(running, pieces):
        total_here, local_here = pieces
        return (jnp.exp(total_here)[:, None, None] * running + local_here, running)
    start_state = jnp.zeros((HEADS, HEAD_DIM, STATE), jnp.float32)
    unused_end, carried = lax.scan(advance, start_state, (block_total, local_state))
    carried_bf = carried.astype(jnp.bfloat16)
    inter = jnp.exp(cumulative)[..., None] * jnp.einsum('btn,bhpn->bthp', query_blk.astype(jnp.float32), carried_bf.astype(jnp.float32))
    ssd_out = inner_part + inter + skip_gain[None, None, :, None] * signal_blk.astype(jnp.float32)
    ssd_out = ssd_out.reshape(TOKEN_COUNT, INNER)
    gated_out = ssd_out * jax.nn.silu(gate_input.astype(jnp.float32))
    squares = lax.optimization_barrier(jnp.sum(gated_out * gated_out, axis=1))
    scaling = 1.0 / jnp.sqrt(squares / INNER + 1e-05)
    gained = (gated_out * norm_gain[None, :]).astype(jnp.bfloat16)
    group_width = INNER // N_MP
    summed = jnp.zeros((TOKEN_COUNT, D), jnp.float32)
    for group_number in range(N_MP):
        lower = group_number * group_width
        partial_value = jnp.dot(gained[:, lower:lower + group_width], out_weight[lower:lower + group_width], preferred_element_type=jnp.float32).astype(jnp.bfloat16)
        partial_value = lax.optimization_barrier(partial_value)
        summed = summed + partial_value.astype(jnp.float32)
    return (scaling[:, None] * summed).astype(jnp.bfloat16)
```

```python
import jax
import jax.numpy as jnp
from jax import lax
from jax.experimental import pallas as pl
from jax.experimental.pallas import tpu as pltpu
from jax.sharding import PartitionSpec as P

SUB = 128
PAIRS = 2
QUAD = 4
RELAY_CHUNKS = 2
FINE = 64
LANES = 128
TILE = 256
LOG2E = 1.4426950408889634
MESH = pl.DeviceIdType.MESH
EXACT = lax.Precision.HIGHEST


def step_target(step, zm, lines):
    up = zm // (lines // 2)
    short = zm * (1 - up) + (lines - 1 - zm) * up
    late = (step + 2 * short) // (lines - 1)
    k = step - (lines - 1 - 2 * short)
    long_side = (1 - late) + late * (k % 2)
    distance = (1 - late) * (lines - 1 - short - step) + late * (short - k // 2)
    seen = short + distance * (2 * long_side - 1)
    return seen * (1 - up) + (lines - 1 - seen) * up


def units_of(tokens):
    half = tokens // 2
    fine = [(r, FINE) for r in range(0, half, FINE)]
    return fine + [(r, SUB) for r in range(half, tokens, SUB)]


def layer_kernel(
    signal_ref,
    gate_ref,
    keys_ref,
    query_ref,
    decay_ref,
    step_ref,
    skip_ref,
    gain_ref,
    weight_ref,
    out_ref,
    gained,
    square_row,
    inner,
    local,
    spread,
    shift,
    cum_cols,
    relay_out,
    relay_in,
    wbuf,
    own,
    from_low,
    from_high,
    total,
    sq_in,
    w_sem,
    wy_send,
    wy_recv,
    wx_send,
    wx_recv,
    wc_send,
    wc_recv,
    wd_send,
    wd_recv,
    a_send,
    a_recv,
    z_send,
    low_recv,
    high_recv,
    sq_send,
    sq_recv,
    relay_send,
    relay_recv,
):
    me = lax.axis_index("mp")
    lines = wbuf.shape[0]
    count = lines * PAIRS
    zm = me // PAIRS
    ym = me % PAIRS
    tokens, depth = signal_ref.shape
    width = out_ref.shape[1]
    parts = width // TILE
    chunks = lines * parts
    quarter = depth // QUAD
    units = units_of(tokens)

    seq = lax.axis_index("seq")
    seq_count = lax.axis_size("seq")
    place = seq % QUAD
    across = (place + 2) % QUAD
    x_peer = {"seq": seq - place + across}
    c_peer = {"seq": seq + 1 - 2 * (seq % 2)}
    y_peer = {"mp": zm * PAIRS + 1 - ym}

    barrier = pltpu.get_barrier_semaphore()
    for d in range(1, count):
        pl.semaphore_signal(
            barrier, inc=1, device_id={"mp": (me + d) % count}, device_id_type=MESH
        )
    for d in (1, seq_count - 1):
        pl.semaphore_signal(
            barrier, inc=1, device_id={"seq": (seq + d) % seq_count}, device_id_type=MESH
        )
    pl.semaphore_signal(barrier, inc=1, device_id=x_peer, device_id_type=MESH)

    def target_of(t):
        last = t // (lines - 1)
        return step_target(t, zm, lines) * (1 - last) + zm * last

    def w_copy(t):
        z = target_of(t)
        cols = pl.ds(pl.multiple_of((z * PAIRS + ym) * width, width), width)
        return pltpu.make_async_copy(
            weight_ref.at[:, cols], wbuf.at[t, pl.ds(0, depth)], w_sem.at[t]
        )

    for t in range(lines):
        w_copy(t).start()

    def rows_of(index):
        return pl.ds(pl.multiple_of(depth + index * quarter, quarter), quarter)

    def cols_of(j):
        return pl.ds(pl.multiple_of((j % parts) * TILE, TILE), TILE)

    def remote(src, dst, send, recv, device):
        return pltpu.make_async_remote_copy(
            src_ref=src,
            dst_ref=dst,
            send_sem=send,
            recv_sem=recv,
            device_id=device,
            device_id_type=MESH,
        )

    def wy_copy(j):
        t = j // parts
        z = target_of(t)
        at = (z * PAIRS + 1 - ym) * width + (j % parts) * TILE
        src = weight_ref.at[
            pl.ds(pl.multiple_of(place * quarter, quarter), quarter),
            pl.ds(pl.multiple_of(at, TILE), TILE),
        ]
        dst = wbuf.at[t, rows_of(place), cols_of(j)]
        return remote(src, dst, wy_send.at[0], wy_recv.at[j], y_peer)

    def spread_copy(j, index, send, recv, device):
        piece = wbuf.at[j // parts, rows_of(index), cols_of(j)]
        return remote(piece, piece, send.at[0], recv.at[j], device)

    def from_y(j):
        spread_copy(j, place, wy_send, wy_recv, y_peer).wait_recv()
        spread_copy(j, place, wx_send, wx_recv, x_peer).start()
        spread_copy(j, place, wc_send, wc_recv, c_peer).start()

    def from_y_next(j):
        from_y(j)

        @pl.when(j + parts < chunks)
        def _():
            wy_copy(j + parts).start()

    def from_x(j):
        spread_copy(j, across, wx_send, wx_recv, x_peer).wait_recv()
        spread_copy(j, across, wd_send, wd_recv, c_peer).start()

    def ensure(j):
        spread_copy(j, place, wc_send, wc_recv, c_peer).wait_recv()
        spread_copy(j, across, wd_send, wd_recv, c_peer).wait_recv()

    pl.semaphore_wait(barrier, count + 2)
    for j in range(parts):
        wy_copy(j).start()

    heads = decay_ref.shape[0]
    head_width = depth // heads
    state_width = keys_ref.shape[1]
    blocks = tokens // SUB
    pair_count = depth // LANES

    def span_of(b):
        return slice(b * SUB, (b + 1) * SUB)

    row_ids = lax.broadcasted_iota(jnp.int32, (SUB, SUB), 0)
    col_ids = lax.broadcasted_iota(jnp.int32, (SUB, SUB), 1)
    upper = jnp.where(row_ids <= col_ids, 1.0, 0.0).astype(jnp.float32)
    stacked_decay = jnp.concatenate([decay_ref[:, span_of(b)] for b in range(blocks)], axis=0)
    stacked_step = jnp.concatenate([step_ref[:, span_of(b)] for b in range(blocks)], axis=0)
    cum = (
        jnp.dot(stacked_decay, upper, precision=EXACT, preferred_element_type=jnp.float32)
        * LOG2E
    )
    feed = stacked_step * jnp.exp2(cum[:, SUB - 1 : SUB] - cum)
    grow = jnp.exp2(cum)
    shift[...] = cum - jnp.log2(stacked_step)

    def split(value):
        high = value.astype(jnp.bfloat16).astype(jnp.float32)
        return [high, value - high]

    slot_ids = lax.broadcasted_iota(jnp.int32, (LANES, depth), 0)
    head_ids = lax.broadcasted_iota(jnp.int32, (LANES, depth), 1) // head_width
    hit = slot_ids % heads == head_ids
    first = slot_ids // (2 * heads)
    pick_feed = jnp.where(jnp.logical_and(hit, first == 0), 1.0, 0.0).astype(jnp.bfloat16)
    pick_grow = jnp.where(jnp.logical_and(hit, first == 1), 1.0, 0.0).astype(jnp.bfloat16)
    filler = jnp.zeros((LANES - 5 * heads, SUB), jnp.float32)
    for b in range(blocks):
        span = span_of(b)
        mine = slice(b * heads, (b + 1) * heads)
        cols = jnp.transpose(
            jnp.concatenate(split(feed[mine]) + split(grow[mine]) + [cum[mine], filler], axis=0)
        )
        cum_cols[b] = cols
        slim = cols.astype(jnp.bfloat16)
        wide_feed = jnp.dot(slim, pick_feed, preferred_element_type=jnp.float32)
        spread[span, :] = jnp.dot(slim, pick_grow, preferred_element_type=jnp.float32)
        feed_rows = (signal_ref[span, :].astype(jnp.float32) * wide_feed).astype(jnp.bfloat16)
        keys_t = jnp.transpose(keys_ref[span, :].astype(jnp.float32)).astype(jnp.bfloat16)
        local[b] = jnp.dot(keys_t, feed_rows, preferred_element_type=jnp.float32)

    def block_decay(b):
        last = (b + 1) * SUB - 1
        return spread[last : last + 1, :]

    def relay_copy(c):
        n = state_width // RELAY_CHUNKS
        part = pl.ds(c * n, n)
        return remote(
            relay_out.at[part],
            relay_in.at[part],
            relay_send.at[c],
            relay_recv.at[c],
            {"seq": (seq + 1) % seq_count},
        )

    @pl.when(seq == 0)
    def _():
        relay_in[...] = jnp.zeros_like(relay_in)

    def relay():
        for c in range(RELAY_CHUNKS):
            n = state_width // RELAY_CHUNKS
            part = slice(c * n, (c + 1) * n)

            @pl.when(seq > 0)
            def _():
                relay_copy(c).wait_recv()

            @pl.when(seq < seq_count - 1)
            def _():
                state = relay_in[part, :].astype(jnp.float32)
                for b in range(blocks):
                    state = block_decay(b) * state + local[b, part, :]
                relay_out[part, :] = state.astype(jnp.bfloat16)
                relay_copy(c).start()

    low_lane = lax.broadcasted_iota(jnp.int32, (SUB, LANES), 1) < head_width
    low_row = lax.broadcasted_iota(jnp.int32, (1, LANES), 1) < head_width
    none = jnp.zeros((SUB, LANES), jnp.bfloat16)

    def inner_block(b):
        span = span_of(b)
        scores = lax.dot_general(
            query_ref[span, :],
            keys_ref[span, :],
            (((1,), (1,)), ((), ())),
            preferred_element_type=jnp.float32,
        )
        scores = jnp.where(row_ids >= col_ids, scores, 0.0)
        for p in range(pair_count):
            cols = slice(p * LANES, (p + 1) * LANES)
            weights = []
            for h in (2 * p, 2 * p + 1):
                at = 4 * heads + h
                gaps = cum_cols[b, :, at : at + 1] - shift[b * heads + h : b * heads + h + 1, :]
                weights.append(
                    (scores * jnp.exp2(jnp.minimum(gaps, 100.0))).astype(jnp.bfloat16)
                )
            pair = signal_ref[span, cols]
            apart = jnp.concatenate(
                [jnp.where(low_lane, pair, none), jnp.where(low_lane, none, pair)], axis=0
            )
            skip = jnp.where(low_row, skip_ref[2 * p], skip_ref[2 * p + 1])
            inner[span, cols] = jnp.dot(
                jnp.concatenate(weights, axis=1), apart, preferred_element_type=jnp.float32
            ) + skip * pair.astype(jnp.float32)

    def gate_block(b, state):
        span = span_of(b)
        carried = state.astype(jnp.bfloat16)
        squared = jnp.zeros((SUB, LANES), jnp.float32)
        for p in range(depth // TILE):
            wide = slice(p * TILE, (p + 1) * TILE)
            read = jnp.dot(query_ref[span, :], carried[:, wide], preferred_element_type=jnp.float32)
            gate = gate_ref[span, wide].astype(jnp.float32)
            half = 0.5 * gate
            gated = (inner[span, wide] + spread[span, wide] * read) * (half + half * jnp.tanh(half))
            both = gated * gated
            squared = squared + both[:, :LANES] + both[:, LANES:]
            gained[span, wide] = (gated * gain_ref[:, wide]).astype(jnp.bfloat16)
        square_row[:, span] = jnp.sum(jnp.transpose(squared), axis=0, keepdims=True)

    def a_copy(u):
        at = pl.ds(*units[u])
        return remote(
            gained.at[at, pl.ds(0, depth)],
            gained.at[at, pl.ds(depth, depth)],
            a_send.at[0],
            a_recv.at[u],
            y_peer,
        )

    def sq_copy(d):
        return remote(
            square_row,
            sq_in.at[me],
            sq_send.at[d],
            sq_recv.at[me],
            {"mp": (me + d) % count},
        )

    def sq_arrival(source):
        return remote(square_row, sq_in.at[source], sq_send.at[0], sq_recv.at[source], y_peer)

    pl.when(seq == 0)(relay)
    inner_block(0)
    pl.when(seq == 1)(relay)
    inner_block(1)
    from_y(0)
    inner_block(2)
    pl.when(seq == 2)(relay)
    inner_block(3)
    for b in range(4, blocks):
        inner_block(b)
    from_y(1)
    pl.when(seq >= 3)(relay)
    from_x(0)

    early = parts // 2
    state = relay_in[...].astype(jnp.float32)
    for b in range(blocks):
        gate_block(b, state)
        for u, (at, size) in enumerate(units):
            if b * SUB <= at < (b + 1) * SUB:
                a_copy(u).start()
        if b < blocks - 1:
            state = block_decay(b) * state + local[b]
        if b == blocks // 2 - 1:
            for j in range(parts, parts + early):
                wy_copy(j).start()
            if parts > 2:
                from_y(2)
            from_x(1)
        if b == blocks - 2:
            for j in range(parts + early, 2 * parts):
                wy_copy(j).start()
    for d in range(1, count):
        sq_copy(d).start()
    for j in range(3, parts):
        from_y(j)
    for j in range(2, parts - 1):
        from_x(j)
    for t in range(lines):
        w_copy(t).wait()

    def z_copy(j, z, unit, at, size, way):
        recv = low_recv if way > 0 else high_recv
        dest = from_low if way > 0 else from_high
        rows, cols = pl.ds(at, size), cols_of(j)
        return remote(
            own.at[j // parts, rows, cols],
            dest.at[z, rows, cols],
            z_send.at[0],
            recv.at[z, j % parts, unit],
            {"mp": (zm + way) * PAIRS + ym},
        )

    def z_arrival(j, z, unit, at, size, way):
        recv = low_recv if way > 0 else high_recv
        dest = from_low if way > 0 else from_high
        piece = dest.at[z, pl.ds(at, size), cols_of(j)]
        return remote(
            piece, piece, z_send.at[0], recv.at[z, j % parts, unit], {"mp": (zm - way) * PAIRS + ym}
        )

    def multiply(j, at, size):
        total[pl.ds(0, size), :] = jnp.dot(
            gained[pl.ds(at, size), :],
            wbuf[j // parts, :, cols_of(j)],
            preferred_element_type=jnp.float32,
        )

    def gather(j, z, unit, at, size, base):
        rows = pl.ds(base, size)

        @pl.when(jnp.logical_and(z >= zm, zm > 0))
        def _():
            z_arrival(j, z, unit, at, size, 1).wait_recv()
            total[rows, :] += from_low[z, pl.ds(at, size), cols_of(j)].astype(jnp.float32)

        @pl.when(jnp.logical_and(z <= zm, zm < lines - 1))
        def _():
            z_arrival(j, z, unit, at, size, -1).wait_recv()
            total[rows, :] += from_high[z, pl.ds(at, size), cols_of(j)].astype(jnp.float32)

        return rows

    def pass_on(j, unit, at, size, base):
        z = target_of(j // parts)
        rows = gather(j, z, unit, at, size, base)
        own[j // parts, pl.ds(at, size), cols_of(j)] = total[rows, :].astype(jnp.bfloat16)

        @pl.when(z > zm)
        def _():
            z_copy(j, z, unit, at, size, 1).start()

        @pl.when(z < zm)
        def _():
            z_copy(j, z, unit, at, size, -1).start()

    def fine_step(j, u):
        at = pl.multiple_of(u * FINE, FINE)
        multiply(j, at, FINE)
        pass_on(j, u, at, FINE, 0)

    def wide_step(j, lo, hi):
        start = units[lo][0]
        multiply(j, start, units[hi - 1][0] + units[hi - 1][1] - start)
        for u in range(lo, hi):
            at, size = units[u]
            pass_on(j, u, at, size, at - start)

    fine = tokens // 2 // FINE
    last_unit = len(units)

    a_copy(0).wait_recv()

    @pl.loop(0, parts)
    def _(j):
        if parts > 2:

            @pl.when(j == parts - 2)
            def _():
                from_x(parts - 1)

        ensure(j)
        fine_step(j, 0)

    for u in range(1, fine):
        a_copy(u).wait_recv()

        @pl.loop(0, parts)
        def _(j):
            fine_step(j, u)

    for j in range(parts, parts + early):
        from_y_next(j)
    from_x(parts)
    for j in range(parts, parts + early):
        ensure(j)
        wide_step(j, 0, fine)
        if j + 1 < parts + early:
            from_x(j + 1)
    a_copy(fine).wait_recv()
    ready = parts + early

    @pl.loop(0, ready)
    def _(j):
        wide_step(j, fine, fine + 1)

    marks = {0: [], 1: [], 2: [], min(4, ready - 1): []}
    marks[0] += [(from_y_next, ready)]
    marks[1] += [(from_y_next, ready + 1)]
    marks[2] += [(from_x, ready)]
    marks[min(4, ready - 1)] += [(from_y_next, ready + 2), (from_x, ready + 1)]
    cuts = sorted(marks)
    for cut, after in zip(cuts, cuts[1:] + [ready]):
        for act, j in marks[cut]:
            act(j)
        if cut == 0:
            for u in range(fine + 1, last_unit):
                a_copy(u).wait_recv()

        @pl.loop(cut, after)
        def _(j):
            wide_step(j, fine + 1, last_unit)

    squares = square_row[...]
    for d in range(1, count):
        source = (me + d) % count
        sq_arrival(source).wait_recv()
        squares = squares + sq_in[source]
    inverse = 1.0 / jnp.sqrt(squares / (count * depth) + 1e-05)
    scaling = jnp.transpose(jnp.broadcast_to(inverse, (LANES, tokens)))
    spread[:, pl.ds(0, LANES)] = scaling

    def ahead(j):
        @pl.when(j + 3 < chunks)
        def _():
            from_y_next(j + 3)

        @pl.when(j + 2 < chunks)
        def _():
            from_x(j + 2)

        ensure(j)

    @pl.loop(ready, (lines - 1) * parts)
    def _(j):
        ahead(j)
        wide_step(j, 0, last_unit)

    @pl.loop((lines - 1) * parts, chunks)
    def _(j):
        ahead(j)
        multiply(j, 0, tokens)
        for u, (at, size) in enumerate(units):
            gather(j, zm, u, at, size, at)
            factor = spread[at : at + size, :LANES]
            for k in range(TILE // LANES):
                cols = pl.ds(pl.multiple_of((j % parts) * TILE + k * LANES, LANES), LANES)
                out_ref[pl.ds(at, size), cols] = (
                    total[at : at + size, k * LANES : (k + 1) * LANES] * factor
                ).astype(jnp.bfloat16)

    sends = wbuf.at[:, pl.ds(0, quarter)]
    for sem in (wy_send, wx_send, wc_send, wd_send):
        remote(sends, sends, sem.at[0], wy_recv.at[0], y_peer).wait_send()
    sends = gained.at[:, pl.ds(0, depth)]
    remote(sends, sends, a_send.at[0], a_recv.at[0], y_peer).wait_send()
    remote(own, own, z_send.at[0], a_recv.at[0], y_peer).wait_send()
    for d in range(1, count):
        sq_copy(d).wait_send()

    @pl.when(seq < seq_count - 1)
    def _():
        for c in range(RELAY_CHUNKS):
            relay_copy(c).wait_send()


def on_device(
    signal,
    gate_input,
    input_map,
    output_map,
    log_decay,
    step_size,
    skip_gain,
    norm_gain,
    out_weight,
):
    tokens, depth = signal.shape
    heads = skip_gain.shape[0]
    state_width = input_map.shape[1]
    count = lax.axis_size("mp")
    lines = count // PAIRS
    width = out_weight.shape[1] // count
    parts = width // TILE
    chunks = lines * parts
    blocks = tokens // SUB
    units = len(units_of(tokens))
    dma = pltpu.SemaphoreType.DMA
    held = lambda n: pltpu.VMEM((n, tokens, width), jnp.bfloat16)
    whole = pl.BlockSpec(memory_space=pltpu.VMEM)
    return pl.pallas_call(
        layer_kernel,
        out_shape=jax.ShapeDtypeStruct((tokens, width), jnp.bfloat16),
        in_specs=[whole] * 6
        + [pl.BlockSpec(memory_space=pltpu.SMEM), whole]
        + [pl.BlockSpec(memory_space=pl.ANY)],
        out_specs=whole,
        scratch_shapes=[
            pltpu.VMEM((tokens, 2 * depth), jnp.bfloat16),
            pltpu.VMEM((1, tokens), jnp.float32),
            pltpu.VMEM((tokens, depth), jnp.float32),
            pltpu.VMEM((blocks, state_width, depth), jnp.float32),
            pltpu.VMEM((tokens, depth), jnp.float32),
            pltpu.VMEM((blocks * heads, SUB), jnp.float32),
            pltpu.VMEM((blocks, SUB, LANES), jnp.float32),
            pltpu.VMEM((state_width, depth), jnp.bfloat16),
            pltpu.VMEM((state_width, depth), jnp.bfloat16),
            pltpu.VMEM((lines, 2 * depth, width), jnp.bfloat16),
            held(lines - 1),
            held(lines),
            held(lines),
            pltpu.VMEM((tokens, TILE), jnp.float32),
            pltpu.VMEM((count, 1, tokens), jnp.float32),
            dma((lines,)),
            dma((1,)),
            dma((chunks,)),
            dma((1,)),
            dma((chunks,)),
            dma((1,)),
            dma((chunks,)),
            dma((1,)),
            dma((chunks,)),
            dma((1,)),
            dma((units,)),
            dma((1,)),
            dma((lines, parts, units)),
            dma((lines, parts, units)),
            dma((count,)),
            dma((count,)),
            dma((RELAY_CHUNKS,)),
            dma((RELAY_CHUNKS,)),
        ],
        compiler_params=pltpu.CompilerParams(
            collective_id=0, has_side_effects=True, vmem_limit_bytes=58 << 20
        ),
        name="layer",
    )(
        signal,
        gate_input,
        input_map,
        output_map,
        jnp.transpose(log_decay),
        jnp.transpose(step_size),
        skip_gain,
        norm_gain[None],
        out_weight,
    )


def solution(mesh):
    placed = (
        P("seq", "mp"),
        P("seq", "mp"),
        P("seq", None),
        P("seq", None),
        P("seq", "mp"),
        P("seq", "mp"),
        P("mp"),
        P("mp"),
        P("mp", None),
    )
    return jax.shard_map(
        on_device, mesh=mesh, in_specs=placed, out_specs=P("seq", "mp"), check_vma=False
    )
```

```python
import jax
import jax.numpy as jnp
from jax import lax
from jax.experimental import pallas as pl
from jax.experimental.pallas import tpu as pltpu
from jax.sharding import PartitionSpec as P

SUB = 128
PAIRS = 2
QUAD = 4
RELAY_CHUNKS = 2
FINE = 64
LANES = 128
TILE = 256
LOG2E = 1.4426950408889634
MESH = pl.DeviceIdType.MESH
EXACT = lax.Precision.HIGHEST


def step_target(step, zm, lines):
    up = zm // (lines // 2)
    short = zm * (1 - up) + (lines - 1 - zm) * up
    late = (step + 2 * short) // (lines - 1)
    k = step - (lines - 1 - 2 * short)
    long_side = (1 - late) + late * (k % 2)
    distance = (1 - late) * (lines - 1 - short - step) + late * (short - k // 2)
    seen = short + distance * (2 * long_side - 1)
    return seen * (1 - up) + (lines - 1 - seen) * up


def units_of(tokens):
    half = tokens // 2
    fine = [(r, FINE) for r in range(SUB, half, FINE)]
    return [(0, SUB)] + fine + [(r, SUB) for r in range(half, tokens, SUB)]


def layer_kernel(
    signal_hbm,
    gate_hbm,
    keys_ref,
    query_ref,
    decay_ref,
    step_ref,
    skip_ref,
    gain_ref,
    weight_ref,
    out_ref,
    signal_ref,
    gate_ref,
    gained,
    square_row,
    inner,
    local,
    spread,
    shift,
    cum_cols,
    relay_out,
    relay_in,
    wbuf,
    own,
    from_low,
    from_high,
    total,
    w_cross,
    cross_out,
    up_in,
    down_in,
    last_in,
    sq_in,
    in_sem,
    w_sem,
    wy_send,
    wy_recv,
    wx_send,
    wx_recv,
    wc_send,
    wc_recv,
    wd_send,
    wd_recv,
    a_send,
    a_recv,
    z_send,
    low_recv,
    high_recv,
    cross_send,
    up_recv,
    down_recv,
    last_recv,
    sq_send,
    sq_recv,
    relay_send,
    relay_recv,
):
    me = lax.axis_index("mp")
    lines = wbuf.shape[0]
    count = lines * PAIRS
    zm = me // PAIRS
    ym = me % PAIRS
    tokens, depth = signal_ref.shape
    width = out_ref.shape[1]
    parts = width // TILE
    chunks = lines * parts
    quarter = depth // QUAD
    units = units_of(tokens)

    seq = lax.axis_index("seq")
    seq_count = lax.axis_size("seq")
    place = seq % QUAD
    across = (place + 2) % QUAD
    x_peer = {"seq": seq - place + across}
    c_peer = {"seq": seq + 1 - 2 * (seq % 2)}
    y_peer = {"mp": zm * PAIRS + 1 - ym}

    barrier = pltpu.get_barrier_semaphore()
    for d in range(1, count):
        pl.semaphore_signal(
            barrier, inc=1, device_id={"mp": (me + d) % count}, device_id_type=MESH
        )
    for d in (1, seq_count - 1):
        pl.semaphore_signal(
            barrier, inc=1, device_id={"seq": (seq + d) % seq_count}, device_id_type=MESH
        )
    pl.semaphore_signal(barrier, inc=1, device_id=x_peer, device_id_type=MESH)

    def target_of(t):
        last = t // (lines - 1)
        return step_target(t, zm, lines) * (1 - last) + zm * last

    def w_copy(t):
        z = target_of(t)
        cols = pl.ds(pl.multiple_of((z * PAIRS + ym) * width, width), width)
        return pltpu.make_async_copy(
            weight_ref.at[:, cols], wbuf.at[t, pl.ds(0, depth)], w_sem.at[t]
        )

    def w_cross_copy():
        cols = pl.ds(pl.multiple_of((target_of(0) * PAIRS + 1 - ym) * width, width), width)
        return pltpu.make_async_copy(weight_ref.at[:, cols], w_cross, w_sem.at[lines])

    signal_copy = pltpu.make_async_copy(signal_hbm, signal_ref, in_sem.at[0])
    gate_copy = pltpu.make_async_copy(gate_hbm, gate_ref, in_sem.at[1])
    signal_copy.start()
    gate_copy.start()

    def rows_of(index):
        return pl.ds(pl.multiple_of(depth + index * quarter, quarter), quarter)

    def cols_of(j):
        return pl.ds(pl.multiple_of((j % parts) * TILE, TILE), TILE)

    def remote(src, dst, send, recv, device):
        return pltpu.make_async_remote_copy(
            src_ref=src,
            dst_ref=dst,
            send_sem=send,
            recv_sem=recv,
            device_id=device,
            device_id_type=MESH,
        )

    def wy_copy(j):
        t = j // parts
        z = target_of(t)
        at = (z * PAIRS + 1 - ym) * width + (j % parts) * TILE
        src = weight_ref.at[
            pl.ds(pl.multiple_of(place * quarter, quarter), quarter),
            pl.ds(pl.multiple_of(at, TILE), TILE),
        ]
        dst = wbuf.at[t, rows_of(place), cols_of(j)]
        return remote(src, dst, wy_send.at[0], wy_recv.at[j], y_peer)

    def spread_copy(j, index, send, recv, device):
        piece = wbuf.at[j // parts, rows_of(index), cols_of(j)]
        return remote(piece, piece, send.at[0], recv.at[j], device)

    def from_y(j):
        spread_copy(j, place, wy_send, wy_recv, y_peer).wait_recv()
        spread_copy(j, place, wx_send, wx_recv, x_peer).start()
        spread_copy(j, place, wc_send, wc_recv, c_peer).start()

    def from_y_next(j):
        from_y(j)

        @pl.when(j + parts < chunks)
        def _():
            wy_copy(j + parts).start()

    def from_x(j):
        spread_copy(j, across, wx_send, wx_recv, x_peer).wait_recv()
        spread_copy(j, across, wd_send, wd_recv, c_peer).start()

    def ensure(j):
        spread_copy(j, place, wc_send, wc_recv, c_peer).wait_recv()
        spread_copy(j, across, wd_send, wd_recv, c_peer).wait_recv()

    pl.semaphore_wait(barrier, count + 2)
    for j in range(parts):
        wy_copy(j).start()
    w_copy(0).start()
    w_cross_copy().start()
    for t in range(1, lines):
        w_copy(t).start()

    heads = decay_ref.shape[0]
    head_width = depth // heads
    state_width = keys_ref.shape[1]
    blocks = tokens // SUB
    pair_count = depth // LANES

    def span_of(b):
        return slice(b * SUB, (b + 1) * SUB)

    row_ids = lax.broadcasted_iota(jnp.int32, (SUB, SUB), 0)
    col_ids = lax.broadcasted_iota(jnp.int32, (SUB, SUB), 1)
    upper = jnp.where(row_ids <= col_ids, 1.0, 0.0).astype(jnp.float32)
    stacked_decay = jnp.concatenate([decay_ref[:, span_of(b)] for b in range(blocks)], axis=0)
    stacked_step = jnp.concatenate([step_ref[:, span_of(b)] for b in range(blocks)], axis=0)
    cum = (
        jnp.dot(stacked_decay, upper, precision=EXACT, preferred_element_type=jnp.float32)
        * LOG2E
    )
    feed = stacked_step * jnp.exp2(cum[:, SUB - 1 : SUB] - cum)
    grow = jnp.exp2(cum)
    shift[...] = cum - jnp.log2(stacked_step)

    def split(value):
        high = value.astype(jnp.bfloat16).astype(jnp.float32)
        return [high, value - high]

    slot_ids = lax.broadcasted_iota(jnp.int32, (LANES, depth), 0)
    head_ids = lax.broadcasted_iota(jnp.int32, (LANES, depth), 1) // head_width
    hit = slot_ids % heads == head_ids
    first = slot_ids // (2 * heads)
    pick_feed = jnp.where(jnp.logical_and(hit, first == 0), 1.0, 0.0).astype(jnp.bfloat16)
    pick_grow = jnp.where(jnp.logical_and(hit, first == 1), 1.0, 0.0).astype(jnp.bfloat16)
    filler = jnp.zeros((LANES - 5 * heads, SUB), jnp.float32)
    signal_copy.wait()
    for b in range(blocks):
        span = span_of(b)
        mine = slice(b * heads, (b + 1) * heads)
        cols = jnp.transpose(
            jnp.concatenate(split(feed[mine]) + split(grow[mine]) + [cum[mine], filler], axis=0)
        )
        cum_cols[b] = cols
        slim = cols.astype(jnp.bfloat16)
        wide_feed = jnp.dot(slim, pick_feed, preferred_element_type=jnp.float32)
        spread[span, :] = jnp.dot(slim, pick_grow, preferred_element_type=jnp.float32)
        feed_rows = (signal_ref[span, :].astype(jnp.float32) * wide_feed).astype(jnp.bfloat16)
        keys_t = jnp.transpose(keys_ref[span, :].astype(jnp.float32)).astype(jnp.bfloat16)
        local[b] = jnp.dot(keys_t, feed_rows, preferred_element_type=jnp.float32)

    def block_decay(b):
        last = (b + 1) * SUB - 1
        return spread[last : last + 1, :]

    def relay_copy(c):
        n = state_width // RELAY_CHUNKS
        part = pl.ds(c * n, n)
        return remote(
            relay_out.at[part],
            relay_in.at[part],
            relay_send.at[c],
            relay_recv.at[c],
            {"seq": (seq + 1) % seq_count},
        )

    @pl.when(seq == 0)
    def _():
        relay_in[...] = jnp.zeros_like(relay_in)

    def relay():
        for c in range(RELAY_CHUNKS):
            n = state_width // RELAY_CHUNKS
            part = slice(c * n, (c + 1) * n)

            @pl.when(seq > 0)
            def _():
                relay_copy(c).wait_recv()

            @pl.when(seq < seq_count - 1)
            def _():
                state = relay_in[part, :].astype(jnp.float32)
                for b in range(blocks):
                    state = block_decay(b) * state + local[b, part, :]
                relay_out[part, :] = state.astype(jnp.bfloat16)
                relay_copy(c).start()

    low_lane = lax.broadcasted_iota(jnp.int32, (SUB, LANES), 1) < head_width
    low_row = lax.broadcasted_iota(jnp.int32, (1, LANES), 1) < head_width
    none = jnp.zeros((SUB, LANES), jnp.bfloat16)

    def inner_block(b):
        span = span_of(b)
        scores = lax.dot_general(
            query_ref[span, :],
            keys_ref[span, :],
            (((1,), (1,)), ((), ())),
            preferred_element_type=jnp.float32,
        )
        scores = jnp.where(row_ids >= col_ids, scores, 0.0)
        for p in range(pair_count):
            cols = slice(p * LANES, (p + 1) * LANES)
            weights = []
            for h in (2 * p, 2 * p + 1):
                at = 4 * heads + h
                gaps = cum_cols[b, :, at : at + 1] - shift[b * heads + h : b * heads + h + 1, :]
                weights.append(
                    (scores * jnp.exp2(jnp.minimum(gaps, 100.0))).astype(jnp.bfloat16)
                )
            pair = signal_ref[span, cols]
            apart = jnp.concatenate(
                [jnp.where(low_lane, pair, none), jnp.where(low_lane, none, pair)], axis=0
            )
            skip = jnp.where(low_row, skip_ref[2 * p], skip_ref[2 * p + 1])
            inner[span, cols] = jnp.dot(
                jnp.concatenate(weights, axis=1), apart, preferred_element_type=jnp.float32
            ) + skip * pair.astype(jnp.float32)

    def gate_block(b, state):
        span = span_of(b)
        carried = state.astype(jnp.bfloat16)
        squared = jnp.zeros((SUB, LANES), jnp.float32)
        for p in range(depth // TILE):
            wide = slice(p * TILE, (p + 1) * TILE)
            read = jnp.dot(query_ref[span, :], carried[:, wide], preferred_element_type=jnp.float32)
            gate = gate_ref[span, wide].astype(jnp.float32)
            half = 0.5 * gate
            gated = (inner[span, wide] + spread[span, wide] * read) * (half + half * jnp.tanh(half))
            both = gated * gated
            squared = squared + both[:, :LANES] + both[:, LANES:]
            gained[span, wide] = (gated * gain_ref[:, wide]).astype(jnp.bfloat16)
        square_row[:, span] = jnp.sum(jnp.transpose(squared), axis=0, keepdims=True)

    def a_copy(u):
        at = pl.ds(*units[u])
        return remote(
            gained.at[at, pl.ds(0, depth)],
            gained.at[at, pl.ds(depth, depth)],
            a_send.at[0],
            a_recv.at[u],
            y_peer,
        )

    def sq_copy(d):
        return remote(
            square_row,
            sq_in.at[me],
            sq_send.at[d],
            sq_recv.at[me],
            {"mp": (me + d) % count},
        )

    def sq_arrival(source):
        return remote(square_row, sq_in.at[source], sq_send.at[0], sq_recv.at[source], y_peer)

    def z_copy(j, z, unit, at, size, way):
        recv = low_recv if way > 0 else high_recv
        dest = from_low if way > 0 else from_high
        rows, cols = pl.ds(at, size), cols_of(j)
        return remote(
            own.at[j // parts, rows, cols],
            dest.at[z, rows, cols],
            z_send.at[0],
            recv.at[z, j % parts, unit],
            {"mp": (zm + way) * PAIRS + ym},
        )

    def z_arrival(j, z, unit, at, size, way):
        recv = low_recv if way > 0 else high_recv
        dest = from_low if way > 0 else from_high
        piece = dest.at[z, pl.ds(at, size), cols_of(j)]
        return remote(
            piece, piece, z_send.at[0], recv.at[z, j % parts, unit], {"mp": (zm - way) * PAIRS + ym}
        )

    def multiply(j, at, size):
        total[pl.ds(0, size), :] = jnp.dot(
            gained[pl.ds(at, size), :],
            wbuf[j // parts, :, cols_of(j)],
            preferred_element_type=jnp.float32,
        )

    def gather(j, z, unit, at, size, base):
        rows = pl.ds(base, size)

        @pl.when(jnp.logical_and(z >= zm, zm > 0))
        def _():
            z_arrival(j, z, unit, at, size, 1).wait_recv()
            total[rows, :] += from_low[z, pl.ds(at, size), cols_of(j)].astype(jnp.float32)

        @pl.when(jnp.logical_and(z <= zm, zm < lines - 1))
        def _():
            z_arrival(j, z, unit, at, size, -1).wait_recv()
            total[rows, :] += from_high[z, pl.ds(at, size), cols_of(j)].astype(jnp.float32)

        return rows

    def pass_on(j, unit, at, size, base):
        z = target_of(j // parts)
        rows = gather(j, z, unit, at, size, base)
        own[j // parts, pl.ds(at, size), cols_of(j)] = total[rows, :].astype(jnp.bfloat16)

        @pl.when(z > zm)
        def _():
            z_copy(j, z, unit, at, size, 1).start()

        @pl.when(z < zm)
        def _():
            z_copy(j, z, unit, at, size, -1).start()

    def wide_step(j, lo, hi):
        start = units[lo][0]
        multiply(j, start, units[hi - 1][0] + units[hi - 1][1] - start)
        for u in range(lo, hi):
            at, size = units[u]
            pass_on(j, u, at, size, at - start)

    lower = zm < lines // 2
    at_end = zm * (lines - 1 - zm) == 0
    inside = zm * (lines - 1 - zm) > 0

    def hop_copy(h, src, dst, recv, device):
        cols = cols_of(h)
        return remote(src.at[:, cols], dst.at[:, cols], cross_send.at[0], recv.at[h], device)

    def line_device(way):
        return {"mp": (zm + way) * PAIRS + ym}

    def first_step(h):
        cols = cols_of(h)
        top = pl.ds(0, SUB)
        own_heads = gained[top, pl.ds(0, depth)]
        total[top, :] = jnp.dot(
            own_heads, wbuf[0, pl.ds(0, depth), cols], preferred_element_type=jnp.float32
        )
        pass_on(h, 0, 0, SUB, 0)
        total[top, :] = jnp.dot(own_heads, w_cross[:, cols], preferred_element_type=jnp.float32)

        @pl.when(jnp.logical_and(lower, zm > 0))
        def _():
            hop_copy(h, up_in, up_in, up_recv, y_peer).wait_recv()
            total[top, :] += up_in[:, cols].astype(jnp.float32)

        @pl.when(jnp.logical_and(zm >= lines // 2, zm < lines - 1))
        def _():
            hop_copy(h, down_in, down_in, down_recv, y_peer).wait_recv()
            total[top, :] += down_in[:, cols].astype(jnp.float32)

        cross_out[:, cols] = total[top, :].astype(jnp.bfloat16)

        @pl.when(lower)
        def _():
            hop_copy(h, cross_out, up_in, up_recv, line_device(1)).start()

        @pl.when(zm >= lines // 2)
        def _():
            hop_copy(h, cross_out, down_in, down_recv, line_device(-1)).start()

    def hand_on(h, last):
        @pl.when(lower)
        def _():
            hop_copy(h, down_in, down_in, down_recv, y_peer).wait_recv()
            if last:
                hop_copy(h, down_in, last_in, last_recv, y_peer).start()
            else:
                hop_copy(h, down_in, down_in, down_recv, line_device(-1)).start()

        @pl.when(zm >= lines // 2)
        def _():
            hop_copy(h, up_in, up_in, up_recv, y_peer).wait_recv()
            if last:
                hop_copy(h, up_in, last_in, last_recv, y_peer).start()
            else:
                hop_copy(h, up_in, up_in, up_recv, line_device(1)).start()

    def first_steps(lo, hi):
        @pl.loop(lo, hi)
        def _(h):
            first_step(h)

    pl.when(seq == 0)(relay)
    inner_block(0)
    pl.when(seq == 1)(relay)
    inner_block(1)
    inner_block(2)
    pl.when(seq == 2)(relay)
    for b in range(3, blocks):
        inner_block(b)
    from_y(0)
    from_y(1)
    pl.when(seq >= 3)(relay)

    gate_copy.wait()
    w_copy(0).wait()
    w_cross_copy().wait()
    early = parts // 2
    ready = parts + early
    last_unit = len(units)
    fine_end = last_unit - tokens // 2 // SUB

    state = relay_in[...].astype(jnp.float32)
    for b in range(blocks):
        gate_block(b, state)
        if b < blocks - 1:
            state = block_decay(b) * state + local[b]
        if b == 0:
            pl.when(at_end)(lambda: first_steps(0, early))
        if b == 1:
            for u in range(1, fine_end):
                a_copy(u).start()
            pl.when(at_end)(lambda: first_steps(early, parts))
            if parts > 2:
                from_y(2)
            from_x(0)
        if b == 2:
            a_copy(fine_end).start()
            for j in range(parts, ready):
                wy_copy(j).start()
            a_copy(0).start()
            for j in range(3, parts):
                from_y(j)
            from_x(1)
    for u in range(fine_end + 1, last_unit):
        a_copy(u).start()
    for j in range(ready, 2 * parts):
        wy_copy(j).start()
    for d in range(1, count):
        sq_copy(d).start()
    for t in range(1, lines):
        w_copy(t).wait()
    for j in range(2, parts - 1):
        from_x(j)
    pl.when(inside)(lambda: first_steps(0, parts))

    for u in range(1, fine_end + 1):
        a_copy(u).wait_recv()

        @pl.loop(0, parts)
        def _(j):
            if u == 1:
                if parts > 2:
                    pl.when(j == parts - 1)(lambda: from_x(parts - 1))
                ensure(j)
            if u == fine_end:
                pl.when(j == parts - 2)(lambda: from_y_next(parts))

                @pl.when(j == parts - 1)
                def _():
                    for k in range(parts + 1, ready):
                        from_y_next(k)

            wide_step(j, u, u + 1)

    from_x(parts)
    for j in range(parts, ready):
        ensure(j)
        wide_step(j, 1, fine_end + 1)
        if j + 1 < ready:
            from_x(j + 1)

    a_copy(0).wait_recv()

    @pl.loop(parts, ready)
    def _(j):
        wide_step(j, 0, 1)

    @pl.when(inside)
    def _():
        for h in range(parts):
            hand_on(h, False)

    for u in range(fine_end + 1, last_unit):
        a_copy(u).wait_recv()
    marks = [(2, ready), (4, ready + 1)]

    @pl.loop(0, ready)
    def _(k):
        for at, j in marks:
            if at < ready:
                pl.when(k == at)(lambda: from_y_next(j))
        wide_step(k, fine_end + 1, last_unit)

    for at, j in marks:
        if at >= ready:
            from_y_next(j)
    from_x(ready)
    from_y_next(ready + 2)
    ensure(ready)
    wide_step(ready, 0, fine_end)
    from_x(ready + 1)
    from_y_next(ready + 3)
    wide_step(ready, fine_end, last_unit)

    squares = square_row[...]
    for d in range(1, count):
        source = (me + d) % count
        sq_arrival(source).wait_recv()
        squares = squares + sq_in[source]
    inverse = 1.0 / jnp.sqrt(squares / (count * depth) + 1e-05)
    scaling = jnp.transpose(jnp.broadcast_to(inverse, (LANES, tokens)))
    spread[:, pl.ds(0, LANES)] = scaling

    def ahead(j):
        pl.when(j == ready + 2)(lambda: from_y_next(j + 2))
        pl.when(j + 1 < chunks)(lambda: from_x(j + 1))
        pl.when(jnp.logical_and(j > ready + 1, j + 3 < chunks))(lambda: from_y_next(j + 3))
        ensure(j)

    @pl.loop(ready + 1, (lines - 1) * parts)
    def _(j):
        @pl.when(jnp.logical_and(at_end, j == (lines - 1) * parts - 2))
        def _():
            for h in range(parts):
                hand_on(h, True)

        ahead(j)
        wide_step(j, 0, last_unit)

    @pl.loop((lines - 1) * parts, chunks)
    def _(j):
        ahead(j)
        multiply(j, 0, tokens)
        for u, (at, size) in enumerate(units):
            gather(j, zm, u, at, size, at)
            if u == 0:

                @pl.when(at_end)
                def _():
                    h = j % parts
                    hop_copy(h, last_in, last_in, last_recv, y_peer).wait_recv()
                    total[:size, :] += last_in[:, cols_of(h)].astype(jnp.float32)

            factor = spread[at : at + size, :LANES]
            for k in range(TILE // LANES):
                cols = pl.ds(pl.multiple_of((j % parts) * TILE + k * LANES, LANES), LANES)
                out_ref[pl.ds(at, size), cols] = (
                    total[at : at + size, k * LANES : (k + 1) * LANES] * factor
                ).astype(jnp.bfloat16)

    sends = wbuf.at[:, pl.ds(0, quarter)]
    for sem in (wy_send, wx_send, wc_send, wd_send):
        remote(sends, sends, sem.at[0], wy_recv.at[0], y_peer).wait_send()
    sends = gained.at[:, pl.ds(0, depth)]
    remote(sends, sends, a_send.at[0], a_recv.at[0], y_peer).wait_send()
    remote(own, own, z_send.at[0], a_recv.at[0], y_peer).wait_send()
    sends = own.at[0, pl.ds(0, 2 * SUB)]
    remote(sends, sends, cross_send.at[0], a_recv.at[0], y_peer).wait_send()
    for d in range(1, count):
        sq_copy(d).wait_send()

    @pl.when(seq < seq_count - 1)
    def _():
        for c in range(RELAY_CHUNKS):
            relay_copy(c).wait_send()


def on_device(
    signal,
    gate_input,
    input_map,
    output_map,
    log_decay,
    step_size,
    skip_gain,
    norm_gain,
    out_weight,
):
    tokens, depth = signal.shape
    heads = skip_gain.shape[0]
    state_width = input_map.shape[1]
    count = lax.axis_size("mp")
    lines = count // PAIRS
    width = out_weight.shape[1] // count
    parts = width // TILE
    chunks = lines * parts
    blocks = tokens // SUB
    units = len(units_of(tokens))
    dma = pltpu.SemaphoreType.DMA
    held = lambda n: pltpu.VMEM((n, tokens, width), jnp.bfloat16)
    whole = pl.BlockSpec(memory_space=pltpu.VMEM)
    return pl.pallas_call(
        layer_kernel,
        out_shape=jax.ShapeDtypeStruct((tokens, width), jnp.bfloat16),
        in_specs=[pl.BlockSpec(memory_space=pl.ANY)] * 2
        + [whole] * 4
        + [pl.BlockSpec(memory_space=pltpu.SMEM), whole]
        + [pl.BlockSpec(memory_space=pl.ANY)],
        out_specs=whole,
        scratch_shapes=[
            pltpu.VMEM((tokens, depth), jnp.bfloat16),
            pltpu.VMEM((tokens, depth), jnp.bfloat16),
            pltpu.VMEM((tokens, 2 * depth), jnp.bfloat16),
            pltpu.VMEM((1, tokens), jnp.float32),
            pltpu.VMEM((tokens, depth), jnp.float32),
            pltpu.VMEM((blocks, state_width, depth), jnp.float32),
            pltpu.VMEM((tokens, depth), jnp.float32),
            pltpu.VMEM((blocks * heads, SUB), jnp.float32),
            pltpu.VMEM((blocks, SUB, LANES), jnp.float32),
            pltpu.VMEM((state_width, depth), jnp.bfloat16),
            pltpu.VMEM((state_width, depth), jnp.bfloat16),
            pltpu.VMEM((lines, 2 * depth, width), jnp.bfloat16),
            held(lines - 1),
            held(lines),
            held(lines),
            pltpu.VMEM((tokens, TILE), jnp.float32),
            pltpu.VMEM((depth, width), jnp.bfloat16),
            pltpu.VMEM((SUB, width), jnp.bfloat16),
            pltpu.VMEM((SUB, width), jnp.bfloat16),
            pltpu.VMEM((SUB, width), jnp.bfloat16),
            pltpu.VMEM((SUB, width), jnp.bfloat16),
            pltpu.VMEM((count, 1, tokens), jnp.float32),
            dma((2,)),
            dma((lines + 1,)),
            dma((1,)),
            dma((chunks,)),
            dma((1,)),
            dma((chunks,)),
            dma((1,)),
            dma((chunks,)),
            dma((1,)),
            dma((chunks,)),
            dma((1,)),
            dma((units,)),
            dma((1,)),
            dma((lines, parts, units)),
            dma((lines, parts, units)),
            dma((1,)),
            dma((parts,)),
            dma((parts,)),
            dma((parts,)),
            dma((count,)),
            dma((count,)),
            dma((RELAY_CHUNKS,)),
            dma((RELAY_CHUNKS,)),
        ],
        compiler_params=pltpu.CompilerParams(
            collective_id=0, has_side_effects=True, vmem_limit_bytes=58 << 20
        ),
        name="layer",
    )(
        signal,
        gate_input,
        input_map,
        output_map,
        jnp.transpose(log_decay),
        jnp.transpose(step_size),
        skip_gain,
        norm_gain[None],
        out_weight,
    )


def solution(mesh):
    placed = (
        P("seq", "mp"),
        P("seq", "mp"),
        P("seq", None),
        P("seq", None),
        P("seq", "mp"),
        P("seq", "mp"),
        P("mp"),
        P("mp"),
        P("mp", None),
    )
    return jax.shard_map(
        on_device, mesh=mesh, in_specs=placed, out_specs=P("seq", "mp"), check_vma=False
    )
```

```python
import jax
import jax.numpy as jnp
from jax import lax
from jax.experimental import pallas as pl
from jax.experimental.pallas import tpu as pltpu
from jax.sharding import PartitionSpec as P

SUB = 128
PAIRS = 2
QUAD = 4
RELAY_CHUNKS = 4
FINE = 64
LANES = 128
TILE = 256
LOG2E = 1.4426950408889634
MESH = pl.DeviceIdType.MESH
EXACT = lax.Precision.HIGHEST


def step_target(step, zm, lines):
    up = zm // (lines // 2)
    short = zm * (1 - up) + (lines - 1 - zm) * up
    late = (step + 2 * short) // (lines - 1)
    k = step - (lines - 1 - 2 * short)
    long_side = (1 - late) + late * (k % 2)
    distance = (1 - late) * (lines - 1 - short - step) + late * (short - k // 2)
    seen = short + distance * (2 * long_side - 1)
    return seen * (1 - up) + (lines - 1 - seen) * up


def units_of(tokens):
    half = tokens // 2
    fine = [(r, FINE) for r in range(SUB, half, FINE)]
    return [(0, SUB)] + fine + [(r, SUB) for r in range(half, tokens, SUB)]


def layer_kernel(
    signal_hbm,
    gate_hbm,
    keys_hbm,
    query_hbm,
    decay_hbm,
    step_hbm,
    skip_ref,
    gain_hbm,
    weight_ref,
    out_hbm,
    out_ref,
    signal_ref,
    gate_ref,
    keys_ref,
    query_ref,
    decay_ref,
    step_ref,
    gain_ref,
    gained,
    square_row,
    inner,
    local,
    spread,
    shift,
    cum_cols,
    relay_out,
    relay_in,
    wbuf,
    own,
    from_low,
    from_high,
    total,
    w_cross,
    cross_out,
    up_in,
    down_in,
    last_in,
    sq_in,
    in_sem,
    out_sem,
    w_sem,
    wy_send,
    wy_recv,
    wx_send,
    wx_recv,
    wc_send,
    wc_recv,
    wd_send,
    wd_recv,
    a_send,
    a_recv,
    z_send,
    low_recv,
    high_recv,
    cross_send,
    up_recv,
    down_recv,
    last_recv,
    sq_send,
    sq_recv,
    relay_send,
    relay_recv,
):
    me = lax.axis_index("mp")
    lines = wbuf.shape[0]
    count = lines * PAIRS
    zm = me // PAIRS
    ym = me % PAIRS
    tokens, depth = signal_ref.shape
    width = out_ref.shape[1]
    parts = width // TILE
    chunks = lines * parts
    quarter = depth // QUAD
    units = units_of(tokens)

    seq = lax.axis_index("seq")
    seq_count = lax.axis_size("seq")
    place = seq % QUAD
    across = (place + 2) % QUAD
    x_peer = {"seq": seq - place + across}
    c_peer = {"seq": seq + 1 - 2 * (seq % 2)}
    y_peer = {"mp": zm * PAIRS + 1 - ym}

    barrier = pltpu.get_barrier_semaphore()
    for d in range(1, count):
        pl.semaphore_signal(
            barrier, inc=1, device_id={"mp": (me + d) % count}, device_id_type=MESH
        )
    for d in (1, seq_count - 1):
        pl.semaphore_signal(
            barrier, inc=1, device_id={"seq": (seq + d) % seq_count}, device_id_type=MESH
        )
    pl.semaphore_signal(barrier, inc=1, device_id=x_peer, device_id_type=MESH)

    def target_of(t):
        last = t // (lines - 1)
        return step_target(t, zm, lines) * (1 - last) + zm * last

    def w_copy(t):
        z = target_of(t)
        cols = pl.ds(pl.multiple_of((z * PAIRS + ym) * width, width), width)
        return pltpu.make_async_copy(
            weight_ref.at[:, cols], wbuf.at[t, pl.ds(0, depth)], w_sem.at[t]
        )

    def w_cross_copy():
        cols = pl.ds(pl.multiple_of((target_of(0) * PAIRS + 1 - ym) * width, width), width)
        return pltpu.make_async_copy(weight_ref.at[:, cols], w_cross, w_sem.at[lines])

    signal_copy = pltpu.make_async_copy(signal_hbm, signal_ref, in_sem.at[0])
    gate_copy = pltpu.make_async_copy(gate_hbm, gate_ref, in_sem.at[1])
    small_copies = [
        pltpu.make_async_copy(src, dst, in_sem.at[2 + k])
        for k, (src, dst) in enumerate(
            (
                (decay_hbm, decay_ref),
                (step_hbm, step_ref),
                (keys_hbm, keys_ref),
                (query_hbm, query_ref),
                (gain_hbm, gain_ref),
            )
        )
    ]
    for copy in small_copies:
        copy.start()
    signal_copy.start()
    gate_copy.start()

    def rows_of(index):
        return pl.ds(pl.multiple_of(depth + index * quarter, quarter), quarter)

    def cols_of(j):
        return pl.ds(pl.multiple_of((j % parts) * TILE, TILE), TILE)

    def remote(src, dst, send, recv, device):
        return pltpu.make_async_remote_copy(
            src_ref=src,
            dst_ref=dst,
            send_sem=send,
            recv_sem=recv,
            device_id=device,
            device_id_type=MESH,
        )

    def wy_copy(j):
        t = j // parts
        z = target_of(t)
        at = (z * PAIRS + 1 - ym) * width + (j % parts) * TILE
        src = weight_ref.at[
            pl.ds(pl.multiple_of(place * quarter, quarter), quarter),
            pl.ds(pl.multiple_of(at, TILE), TILE),
        ]
        dst = wbuf.at[t, rows_of(place), cols_of(j)]
        return remote(src, dst, wy_send.at[0], wy_recv.at[j], y_peer)

    def spread_copy(j, index, send, recv, device):
        piece = wbuf.at[j // parts, rows_of(index), cols_of(j)]
        return remote(piece, piece, send.at[0], recv.at[j], device)

    def from_y(j):
        spread_copy(j, place, wy_send, wy_recv, y_peer).wait_recv()
        spread_copy(j, place, wx_send, wx_recv, x_peer).start()
        spread_copy(j, place, wc_send, wc_recv, c_peer).start()

    def from_y_next(j):
        from_y(j)

        @pl.when(j + parts < chunks)
        def _():
            wy_copy(j + parts).start()

    def from_x(j):
        spread_copy(j, across, wx_send, wx_recv, x_peer).wait_recv()
        spread_copy(j, across, wd_send, wd_recv, c_peer).start()

    def ensure(j):
        spread_copy(j, place, wc_send, wc_recv, c_peer).wait_recv()
        spread_copy(j, across, wd_send, wd_recv, c_peer).wait_recv()

    pl.semaphore_wait(barrier, count + 2)
    for j in range(parts):
        wy_copy(j).start()
    w_copy(0).start()
    w_cross_copy().start()
    for t in range(1, lines):
        w_copy(t).start()

    heads = decay_ref.shape[0]
    head_width = depth // heads
    state_width = keys_ref.shape[1]
    blocks = tokens // SUB
    pair_count = depth // LANES

    def span_of(b):
        return slice(b * SUB, (b + 1) * SUB)

    for copy in small_copies:
        copy.wait()
    row_ids = lax.broadcasted_iota(jnp.int32, (SUB, SUB), 0)
    col_ids = lax.broadcasted_iota(jnp.int32, (SUB, SUB), 1)
    upper = jnp.where(row_ids <= col_ids, 1.0, 0.0).astype(jnp.float32)
    stacked_decay = jnp.concatenate([decay_ref[:, span_of(b)] for b in range(blocks)], axis=0)
    stacked_step = jnp.concatenate([step_ref[:, span_of(b)] for b in range(blocks)], axis=0)
    cum = (
        jnp.dot(stacked_decay, upper, precision=EXACT, preferred_element_type=jnp.float32)
        * LOG2E
    )
    feed = stacked_step * jnp.exp2(cum[:, SUB - 1 : SUB] - cum)
    grow = jnp.exp2(cum)
    shift[...] = cum - jnp.log2(stacked_step)

    def split(value):
        high = value.astype(jnp.bfloat16).astype(jnp.float32)
        return [high, value - high]

    slot_ids = lax.broadcasted_iota(jnp.int32, (LANES, depth), 0)
    head_ids = lax.broadcasted_iota(jnp.int32, (LANES, depth), 1) // head_width
    hit = slot_ids % heads == head_ids
    first = slot_ids // (2 * heads)
    pick_feed = jnp.where(jnp.logical_and(hit, first == 0), 1.0, 0.0).astype(jnp.bfloat16)
    pick_grow = jnp.where(jnp.logical_and(hit, first == 1), 1.0, 0.0).astype(jnp.bfloat16)
    filler = jnp.zeros((LANES - 5 * heads, SUB), jnp.float32)
    signal_copy.wait()
    for b in range(blocks):
        span = span_of(b)
        mine = slice(b * heads, (b + 1) * heads)
        cols = jnp.transpose(
            jnp.concatenate(split(feed[mine]) + split(grow[mine]) + [cum[mine], filler], axis=0)
        )
        cum_cols[b] = cols
        slim = cols.astype(jnp.bfloat16)
        wide_feed = jnp.dot(slim, pick_feed, preferred_element_type=jnp.float32)
        spread[span, :] = jnp.dot(slim, pick_grow, preferred_element_type=jnp.float32)
        feed_rows = (signal_ref[span, :].astype(jnp.float32) * wide_feed).astype(jnp.bfloat16)
        keys_t = jnp.transpose(keys_ref[span, :].astype(jnp.float32)).astype(jnp.bfloat16)
        local[b] = jnp.dot(keys_t, feed_rows, preferred_element_type=jnp.float32)

    def block_decay(b):
        last = (b + 1) * SUB - 1
        return spread[last : last + 1, :]

    def relay_copy(c):
        n = state_width // RELAY_CHUNKS
        part = pl.ds(c * n, n)
        return remote(
            relay_out.at[part],
            relay_in.at[part],
            relay_send.at[c],
            relay_recv.at[c],
            {"seq": (seq + 1) % seq_count},
        )

    @pl.when(seq == 0)
    def _():
        relay_in[...] = jnp.zeros_like(relay_in)

    def relay():
        for c in range(RELAY_CHUNKS):
            n = state_width // RELAY_CHUNKS
            part = slice(c * n, (c + 1) * n)

            @pl.when(seq > 0)
            def _():
                relay_copy(c).wait_recv()

            @pl.when(seq < seq_count - 1)
            def _():
                state = relay_in[part, :].astype(jnp.float32)
                for b in range(blocks):
                    state = block_decay(b) * state + local[b, part, :]
                relay_out[part, :] = state.astype(jnp.bfloat16)
                relay_copy(c).start()

    low_lane = lax.broadcasted_iota(jnp.int32, (SUB, LANES), 1) < head_width
    low_row = lax.broadcasted_iota(jnp.int32, (1, LANES), 1) < head_width
    none = jnp.zeros((SUB, LANES), jnp.bfloat16)

    def inner_block(b):
        span = span_of(b)
        scores = lax.dot_general(
            query_ref[span, :],
            keys_ref[span, :],
            (((1,), (1,)), ((), ())),
            preferred_element_type=jnp.float32,
        )
        scores = jnp.where(row_ids >= col_ids, scores, 0.0)
        for p in range(pair_count):
            cols = slice(p * LANES, (p + 1) * LANES)
            weights = []
            for h in (2 * p, 2 * p + 1):
                at = 4 * heads + h
                gaps = cum_cols[b, :, at : at + 1] - shift[b * heads + h : b * heads + h + 1, :]
                weights.append(
                    (scores * jnp.exp2(jnp.minimum(gaps, 100.0))).astype(jnp.bfloat16)
                )
            pair = signal_ref[span, cols]
            apart = jnp.concatenate(
                [jnp.where(low_lane, pair, none), jnp.where(low_lane, none, pair)], axis=0
            )
            skip = jnp.where(low_row, skip_ref[2 * p], skip_ref[2 * p + 1])
            inner[span, cols] = jnp.dot(
                jnp.concatenate(weights, axis=1), apart, preferred_element_type=jnp.float32
            ) + skip * pair.astype(jnp.float32)

    def gate_block(b, state):
        span = span_of(b)
        carried = state.astype(jnp.bfloat16)
        squared = jnp.zeros((SUB, LANES), jnp.float32)
        for p in range(depth // TILE):
            wide = slice(p * TILE, (p + 1) * TILE)
            read = jnp.dot(query_ref[span, :], carried[:, wide], preferred_element_type=jnp.float32)
            gate = gate_ref[span, wide].astype(jnp.float32)
            half = 0.5 * gate
            gated = (inner[span, wide] + spread[span, wide] * read) * (half + half * jnp.tanh(half))
            both = gated * gated
            squared = squared + both[:, :LANES] + both[:, LANES:]
            gained[span, wide] = (gated * gain_ref[:, wide]).astype(jnp.bfloat16)
        square_row[:, span] = jnp.sum(jnp.transpose(squared), axis=0, keepdims=True)

    def a_copy(u):
        at = pl.ds(*units[u])
        return remote(
            gained.at[at, pl.ds(0, depth)],
            gained.at[at, pl.ds(depth, depth)],
            a_send.at[0],
            a_recv.at[u],
            y_peer,
        )

    def sq_copy(d):
        return remote(
            square_row,
            sq_in.at[me],
            sq_send.at[d],
            sq_recv.at[me],
            {"mp": (me + d) % count},
        )

    def sq_arrival(source):
        return remote(square_row, sq_in.at[source], sq_send.at[0], sq_recv.at[source], y_peer)

    def z_copy(j, z, unit, at, size, way):
        recv = low_recv if way > 0 else high_recv
        dest = from_low if way > 0 else from_high
        rows, cols = pl.ds(at, size), cols_of(j)
        return remote(
            own.at[j // parts, rows, cols],
            dest.at[z, rows, cols],
            z_send.at[0],
            recv.at[z, j % parts, unit],
            {"mp": (zm + way) * PAIRS + ym},
        )

    def z_arrival(j, z, unit, at, size, way):
        recv = low_recv if way > 0 else high_recv
        dest = from_low if way > 0 else from_high
        piece = dest.at[z, pl.ds(at, size), cols_of(j)]
        return remote(
            piece, piece, z_send.at[0], recv.at[z, j % parts, unit], {"mp": (zm - way) * PAIRS + ym}
        )

    def multiply(j, at, size):
        total[pl.ds(0, size), :] = jnp.dot(
            gained[pl.ds(at, size), :],
            wbuf[j // parts, :, cols_of(j)],
            preferred_element_type=jnp.float32,
        )

    def gather(j, z, unit, at, size, base):
        rows = pl.ds(base, size)

        @pl.when(jnp.logical_and(z >= zm, zm > 0))
        def _():
            z_arrival(j, z, unit, at, size, 1).wait_recv()
            total[rows, :] += from_low[z, pl.ds(at, size), cols_of(j)].astype(jnp.float32)

        @pl.when(jnp.logical_and(z <= zm, zm < lines - 1))
        def _():
            z_arrival(j, z, unit, at, size, -1).wait_recv()
            total[rows, :] += from_high[z, pl.ds(at, size), cols_of(j)].astype(jnp.float32)

        return rows

    def pass_on(j, unit, at, size, base):
        z = target_of(j // parts)
        rows = gather(j, z, unit, at, size, base)
        own[j // parts, pl.ds(at, size), cols_of(j)] = total[rows, :].astype(jnp.bfloat16)

        @pl.when(z > zm)
        def _():
            z_copy(j, z, unit, at, size, 1).start()

        @pl.when(z < zm)
        def _():
            z_copy(j, z, unit, at, size, -1).start()

    def wide_step(j, lo, hi):
        start = units[lo][0]
        multiply(j, start, units[hi - 1][0] + units[hi - 1][1] - start)
        for u in range(lo, hi):
            at, size = units[u]
            pass_on(j, u, at, size, at - start)

    lower = zm < lines // 2
    at_end = zm * (lines - 1 - zm) == 0
    inside = zm * (lines - 1 - zm) > 0

    def hop_copy(h, src, dst, recv, device):
        cols = cols_of(h)
        return remote(src.at[:, cols], dst.at[:, cols], cross_send.at[0], recv.at[h], device)

    def line_device(way):
        return {"mp": (zm + way) * PAIRS + ym}

    def first_step(h):
        cols = cols_of(h)
        top = pl.ds(0, SUB)
        own_heads = gained[top, pl.ds(0, depth)]
        total[top, :] = jnp.dot(
            own_heads, wbuf[0, pl.ds(0, depth), cols], preferred_element_type=jnp.float32
        )
        pass_on(h, 0, 0, SUB, 0)
        total[top, :] = jnp.dot(own_heads, w_cross[:, cols], preferred_element_type=jnp.float32)

        @pl.when(jnp.logical_and(lower, zm > 0))
        def _():
            hop_copy(h, up_in, up_in, up_recv, y_peer).wait_recv()
            total[top, :] += up_in[:, cols].astype(jnp.float32)

        @pl.when(jnp.logical_and(zm >= lines // 2, zm < lines - 1))
        def _():
            hop_copy(h, down_in, down_in, down_recv, y_peer).wait_recv()
            total[top, :] += down_in[:, cols].astype(jnp.float32)

        cross_out[:, cols] = total[top, :].astype(jnp.bfloat16)

        @pl.when(lower)
        def _():
            hop_copy(h, cross_out, up_in, up_recv, line_device(1)).start()

        @pl.when(zm >= lines // 2)
        def _():
            hop_copy(h, cross_out, down_in, down_recv, line_device(-1)).start()

    def hand_on(h, last):
        @pl.when(lower)
        def _():
            hop_copy(h, down_in, down_in, down_recv, y_peer).wait_recv()
            if last:
                hop_copy(h, down_in, last_in, last_recv, y_peer).start()
            else:
                hop_copy(h, down_in, down_in, down_recv, line_device(-1)).start()

        @pl.when(zm >= lines // 2)
        def _():
            hop_copy(h, up_in, up_in, up_recv, y_peer).wait_recv()
            if last:
                hop_copy(h, up_in, last_in, last_recv, y_peer).start()
            else:
                hop_copy(h, up_in, up_in, up_recv, line_device(1)).start()

    def first_steps(lo, hi):
        @pl.loop(lo, hi)
        def _(h):
            first_step(h)

    pl.when(seq == 0)(relay)
    inner_block(0)
    pl.when(seq == 1)(relay)
    inner_block(1)
    inner_block(2)
    pl.when(seq == 2)(relay)
    for b in range(3, blocks):
        inner_block(b)
    from_y(0)
    from_y(1)
    pl.when(seq >= 3)(relay)

    gate_copy.wait()
    w_copy(0).wait()
    w_cross_copy().wait()
    early = parts // 2
    ready = parts + early
    last_unit = len(units)
    fine_end = last_unit - tokens // 2 // SUB

    state = relay_in[...].astype(jnp.float32)
    for b in range(blocks):
        gate_block(b, state)
        if b < blocks - 1:
            state = block_decay(b) * state + local[b]
        if b == 0:
            pl.when(at_end)(lambda: first_steps(0, early))
        if b == 1:
            for u in range(1, fine_end):
                a_copy(u).start()
            pl.when(at_end)(lambda: first_steps(early, parts))
            if parts > 2:
                from_y(2)
            from_x(0)
        if b == 2:
            a_copy(fine_end).start()
            for j in range(parts, ready):
                wy_copy(j).start()
            a_copy(0).start()
            for j in range(3, parts):
                from_y(j)
            from_x(1)
    for u in range(fine_end + 1, last_unit):
        a_copy(u).start()
    for j in range(ready, 2 * parts):
        wy_copy(j).start()
    for d in range(1, count):
        sq_copy(d).start()
    for t in range(1, lines):
        w_copy(t).wait()
    for j in range(2, parts - 1):
        from_x(j)
    pl.when(inside)(lambda: first_steps(0, parts))

    for u in range(1, fine_end + 1):
        a_copy(u).wait_recv()

        @pl.loop(0, parts)
        def _(j):
            if u == 1:
                if parts > 2:
                    pl.when(j == parts - 1)(lambda: from_x(parts - 1))
                ensure(j)
            if u == fine_end:
                pl.when(j == parts - 2)(lambda: from_y_next(parts))

                @pl.when(j == parts - 1)
                def _():
                    for k in range(parts + 1, ready):
                        from_y_next(k)

            wide_step(j, u, u + 1)

    from_x(parts)
    for j in range(parts, ready):
        ensure(j)
        wide_step(j, 1, fine_end + 1)
        if j + 1 < ready:
            from_x(j + 1)

    a_copy(0).wait_recv()

    @pl.loop(parts, ready)
    def _(j):
        wide_step(j, 0, 1)

    @pl.when(inside)
    def _():
        for h in range(parts):
            hand_on(h, False)

    for u in range(fine_end + 1, last_unit):
        a_copy(u).wait_recv()
    marks = [(2, ready), (4, ready + 1)]

    @pl.loop(0, ready)
    def _(k):
        for at, j in marks:
            if at < ready:
                pl.when(k == at)(lambda: from_y_next(j))
        wide_step(k, fine_end + 1, last_unit)

    for at, j in marks:
        if at >= ready:
            from_y_next(j)
    from_x(ready)
    from_y_next(ready + 2)
    ensure(ready)
    wide_step(ready, 0, fine_end)
    from_x(ready + 1)
    from_y_next(ready + 3)
    wide_step(ready, fine_end, last_unit)

    squares = square_row[...]
    for d in range(1, count):
        source = (me + d) % count
        sq_arrival(source).wait_recv()
        squares = squares + sq_in[source]
    inverse = 1.0 / jnp.sqrt(squares / (count * depth) + 1e-05)
    scaling = jnp.transpose(jnp.broadcast_to(inverse, (LANES, tokens)))
    spread[:, pl.ds(0, LANES)] = scaling

    def out_copy(j, u):
        rows, cols = pl.ds(*units[u]), cols_of(j)
        return pltpu.make_async_copy(
            out_ref.at[rows, cols], out_hbm.at[rows, cols], out_sem.at[j % parts, u]
        )

    def ahead(j):
        pl.when(j == ready + 2)(lambda: from_y_next(j + 2))
        pl.when(j + 1 < chunks)(lambda: from_x(j + 1))
        pl.when(jnp.logical_and(j > ready + 1, j + 3 < chunks))(lambda: from_y_next(j + 3))
        ensure(j)

    @pl.loop(ready + 1, (lines - 1) * parts)
    def _(j):
        @pl.when(jnp.logical_and(at_end, j == (lines - 1) * parts - 2))
        def _():
            for h in range(parts):
                hand_on(h, True)

        ahead(j)
        wide_step(j, 0, last_unit)

    @pl.loop((lines - 1) * parts, chunks)
    def _(j):
        ahead(j)
        multiply(j, 0, tokens)
        for u, (at, size) in enumerate(units):
            gather(j, zm, u, at, size, at)
            if u == 0:

                @pl.when(at_end)
                def _():
                    h = j % parts
                    hop_copy(h, last_in, last_in, last_recv, y_peer).wait_recv()
                    total[:size, :] += last_in[:, cols_of(h)].astype(jnp.float32)

            factor = spread[at : at + size, :LANES]
            for k in range(TILE // LANES):
                cols = pl.ds(pl.multiple_of((j % parts) * TILE + k * LANES, LANES), LANES)
                out_ref[pl.ds(at, size), cols] = (
                    total[at : at + size, k * LANES : (k + 1) * LANES] * factor
                ).astype(jnp.bfloat16)
            out_copy(j, u).start()

    for j in range(parts):
        for u in range(last_unit):
            out_copy(j, u).wait()
    sends = wbuf.at[:, pl.ds(0, quarter)]
    for sem in (wy_send, wx_send, wc_send, wd_send):
        remote(sends, sends, sem.at[0], wy_recv.at[0], y_peer).wait_send()
    sends = gained.at[:, pl.ds(0, depth)]
    remote(sends, sends, a_send.at[0], a_recv.at[0], y_peer).wait_send()
    remote(own, own, z_send.at[0], a_recv.at[0], y_peer).wait_send()
    sends = own.at[0, pl.ds(0, 2 * SUB)]
    remote(sends, sends, cross_send.at[0], a_recv.at[0], y_peer).wait_send()
    for d in range(1, count):
        sq_copy(d).wait_send()

    @pl.when(seq < seq_count - 1)
    def _():
        for c in range(RELAY_CHUNKS):
            relay_copy(c).wait_send()


def on_device(
    signal,
    gate_input,
    input_map,
    output_map,
    log_decay,
    step_size,
    skip_gain,
    norm_gain,
    out_weight,
):
    tokens, depth = signal.shape
    heads = skip_gain.shape[0]
    state_width = input_map.shape[1]
    count = lax.axis_size("mp")
    lines = count // PAIRS
    width = out_weight.shape[1] // count
    parts = width // TILE
    chunks = lines * parts
    blocks = tokens // SUB
    units = len(units_of(tokens))
    dma = pltpu.SemaphoreType.DMA
    held = lambda n: pltpu.VMEM((n, tokens, width), jnp.bfloat16)
    anywhere = pl.BlockSpec(memory_space=pl.ANY)
    return pl.pallas_call(
        layer_kernel,
        out_shape=jax.ShapeDtypeStruct((tokens, width), jnp.bfloat16),
        in_specs=[anywhere] * 6
        + [pl.BlockSpec(memory_space=pltpu.SMEM)]
        + [anywhere] * 2,
        out_specs=anywhere,
        scratch_shapes=[
            pltpu.VMEM((tokens, width), jnp.bfloat16),
            pltpu.VMEM((tokens, depth), jnp.bfloat16),
            pltpu.VMEM((tokens, depth), jnp.bfloat16),
            pltpu.VMEM((tokens, state_width), jnp.bfloat16),
            pltpu.VMEM((tokens, state_width), jnp.bfloat16),
            pltpu.VMEM((heads, tokens), jnp.float32),
            pltpu.VMEM((heads, tokens), jnp.float32),
            pltpu.VMEM((1, depth), jnp.float32),
            pltpu.VMEM((tokens, 2 * depth), jnp.bfloat16),
            pltpu.VMEM((1, tokens), jnp.float32),
            pltpu.VMEM((tokens, depth), jnp.float32),
            pltpu.VMEM((blocks, state_width, depth), jnp.float32),
            pltpu.VMEM((tokens, depth), jnp.float32),
            pltpu.VMEM((blocks * heads, SUB), jnp.float32),
            pltpu.VMEM((blocks, SUB, LANES), jnp.float32),
            pltpu.VMEM((state_width, depth), jnp.bfloat16),
            pltpu.VMEM((state_width, depth), jnp.bfloat16),
            pltpu.VMEM((lines, 2 * depth, width), jnp.bfloat16),
            held(lines - 1),
            held(lines),
            held(lines),
            pltpu.VMEM((tokens, TILE), jnp.float32),
            pltpu.VMEM((depth, width), jnp.bfloat16),
            pltpu.VMEM((SUB, width), jnp.bfloat16),
            pltpu.VMEM((SUB, width), jnp.bfloat16),
            pltpu.VMEM((SUB, width), jnp.bfloat16),
            pltpu.VMEM((SUB, width), jnp.bfloat16),
            pltpu.VMEM((count, 1, tokens), jnp.float32),
            dma((7,)),
            dma((parts, units)),
            dma((lines + 1,)),
            dma((1,)),
            dma((chunks,)),
            dma((1,)),
            dma((chunks,)),
            dma((1,)),
            dma((chunks,)),
            dma((1,)),
            dma((chunks,)),
            dma((1,)),
            dma((units,)),
            dma((1,)),
            dma((lines, parts, units)),
            dma((lines, parts, units)),
            dma((1,)),
            dma((parts,)),
            dma((parts,)),
            dma((parts,)),
            dma((count,)),
            dma((count,)),
            dma((RELAY_CHUNKS,)),
            dma((RELAY_CHUNKS,)),
        ],
        compiler_params=pltpu.CompilerParams(
            collective_id=0, has_side_effects=True, vmem_limit_bytes=58 << 20
        ),
        name="layer",
    )(
        signal,
        gate_input,
        input_map,
        output_map,
        jnp.transpose(log_decay),
        jnp.transpose(step_size),
        skip_gain,
        norm_gain[None],
        out_weight,
    )


def solution(mesh):
    placed = (
        P("seq", "mp"),
        P("seq", "mp"),
        P("seq", None),
        P("seq", None),
        P("seq", "mp"),
        P("seq", "mp"),
        P("mp"),
        P("mp"),
        P("mp", None),
    )
    return jax.shard_map(
        on_device, mesh=mesh, in_specs=placed, out_specs=P("seq", "mp"), check_vma=False
    )
```

```python
import jax
import jax.numpy as jnp
from jax import lax
from jax.experimental import pallas as pl
from jax.experimental.pallas import tpu as pltpu
from jax.sharding import PartitionSpec as P

SUB = 128
PAIRS = 2
QUAD = 4
RELAY_CHUNKS = 4
FINE = 128
LANES = 128
TILE = 256
LOG2E = 1.4426950408889634
MESH = pl.DeviceIdType.MESH
EXACT = lax.Precision.HIGHEST


def step_target(step, zm, lines):
    up = zm // (lines // 2)
    short = zm * (1 - up) + (lines - 1 - zm) * up
    late = (step + 2 * short) // (lines - 1)
    k = step - (lines - 1 - 2 * short)
    long_side = (1 - late) + late * (k % 2)
    distance = (1 - late) * (lines - 1 - short - step) + late * (short - k // 2)
    seen = short + distance * (2 * long_side - 1)
    return seen * (1 - up) + (lines - 1 - seen) * up


def units_of(tokens):
    half = tokens // 2
    fine = [(r, FINE) for r in range(SUB, half, FINE)]
    return [(0, SUB)] + fine + [(r, SUB) for r in range(half, tokens, SUB)]


def layer_kernel(
    signal_hbm,
    gate_hbm,
    keys_hbm,
    query_hbm,
    decay_hbm,
    step_hbm,
    skip_ref,
    gain_hbm,
    weight_ref,
    out_hbm,
    out_ref,
    signal_ref,
    gate_ref,
    keys_ref,
    query_ref,
    decay_ref,
    step_ref,
    gain_ref,
    gained,
    square_row,
    inner,
    local,
    spread,
    shift,
    cum_cols,
    relay_out,
    relay_in,
    wbuf,
    own,
    from_low,
    from_high,
    total,
    w_cross,
    cross_out,
    up_in,
    down_in,
    last_in,
    sq_in,
    in_sem,
    out_sem,
    w_sem,
    wy_send,
    wy_recv,
    wx_send,
    wx_recv,
    wc_send,
    wc_recv,
    wd_send,
    wd_recv,
    a_send,
    a_recv,
    z_send,
    low_recv,
    high_recv,
    cross_send,
    up_recv,
    down_recv,
    last_recv,
    sq_send,
    sq_recv,
    relay_send,
    relay_recv,
):
    me = lax.axis_index("mp")
    lines = wbuf.shape[0]
    count = lines * PAIRS
    zm = me // PAIRS
    ym = me % PAIRS
    tokens, depth = signal_ref.shape
    width = out_ref.shape[1]
    parts = width // TILE
    chunks = lines * parts
    quarter = depth // QUAD
    units = units_of(tokens)

    seq = lax.axis_index("seq")
    seq_count = lax.axis_size("seq")
    place = seq % QUAD
    across = (place + 2) % QUAD
    x_peer = {"seq": seq - place + across}
    c_peer = {"seq": seq + 1 - 2 * (seq % 2)}
    y_peer = {"mp": zm * PAIRS + 1 - ym}

    barrier = pltpu.get_barrier_semaphore()
    for d in range(1, count):
        pl.semaphore_signal(
            barrier, inc=1, device_id={"mp": (me + d) % count}, device_id_type=MESH
        )
    for d in (1, seq_count - 1):
        pl.semaphore_signal(
            barrier, inc=1, device_id={"seq": (seq + d) % seq_count}, device_id_type=MESH
        )
    pl.semaphore_signal(barrier, inc=1, device_id=x_peer, device_id_type=MESH)

    def target_of(t):
        last = t // (lines - 1)
        return step_target(t, zm, lines) * (1 - last) + zm * last

    def w_copy(t):
        z = target_of(t)
        cols = pl.ds(pl.multiple_of((z * PAIRS + ym) * width, width), width)
        return pltpu.make_async_copy(
            weight_ref.at[:, cols], wbuf.at[t, pl.ds(0, depth)], w_sem.at[t]
        )

    def w_cross_copy():
        cols = pl.ds(pl.multiple_of((target_of(0) * PAIRS + 1 - ym) * width, width), width)
        return pltpu.make_async_copy(weight_ref.at[:, cols], w_cross, w_sem.at[lines])

    signal_copy = pltpu.make_async_copy(signal_hbm, signal_ref, in_sem.at[0])
    gate_copy = pltpu.make_async_copy(gate_hbm, gate_ref, in_sem.at[1])
    small_copies = [
        pltpu.make_async_copy(src, dst, in_sem.at[2 + k])
        for k, (src, dst) in enumerate(
            (
                (decay_hbm, decay_ref),
                (step_hbm, step_ref),
                (keys_hbm, keys_ref),
                (query_hbm, query_ref),
                (gain_hbm, gain_ref),
            )
        )
    ]
    for copy in small_copies:
        copy.start()
    signal_copy.start()
    gate_copy.start()

    def rows_of(index):
        return pl.ds(pl.multiple_of(depth + index * quarter, quarter), quarter)

    def cols_of(j):
        return pl.ds(pl.multiple_of((j % parts) * TILE, TILE), TILE)

    def remote(src, dst, send, recv, device):
        return pltpu.make_async_remote_copy(
            src_ref=src,
            dst_ref=dst,
            send_sem=send,
            recv_sem=recv,
            device_id=device,
            device_id_type=MESH,
        )

    def wy_copy(j):
        t = j // parts
        z = target_of(t)
        at = (z * PAIRS + 1 - ym) * width + (j % parts) * TILE
        src = weight_ref.at[
            pl.ds(pl.multiple_of(place * quarter, quarter), quarter),
            pl.ds(pl.multiple_of(at, TILE), TILE),
        ]
        dst = wbuf.at[t, rows_of(place), cols_of(j)]
        return remote(src, dst, wy_send.at[0], wy_recv.at[j], y_peer)

    def spread_copy(j, index, send, recv, device):
        piece = wbuf.at[j // parts, rows_of(index), cols_of(j)]
        return remote(piece, piece, send.at[0], recv.at[j], device)

    def from_y(j):
        spread_copy(j, place, wy_send, wy_recv, y_peer).wait_recv()
        spread_copy(j, place, wx_send, wx_recv, x_peer).start()
        spread_copy(j, place, wc_send, wc_recv, c_peer).start()

    def from_y_next(j):
        from_y(j)

        @pl.when(j + parts < chunks)
        def _():
            wy_copy(j + parts).start()

    def from_x(j):
        spread_copy(j, across, wx_send, wx_recv, x_peer).wait_recv()
        spread_copy(j, across, wd_send, wd_recv, c_peer).start()

    def ensure(j):
        spread_copy(j, place, wc_send, wc_recv, c_peer).wait_recv()
        spread_copy(j, across, wd_send, wd_recv, c_peer).wait_recv()

    pl.semaphore_wait(barrier, count + 2)
    for j in range(parts):
        wy_copy(j).start()
    w_copy(0).start()
    w_cross_copy().start()
    for t in range(1, lines):
        w_copy(t).start()

    heads = decay_ref.shape[0]
    head_width = depth // heads
    state_width = keys_ref.shape[1]
    blocks = tokens // SUB
    pair_count = depth // LANES

    def span_of(b):
        return slice(b * SUB, (b + 1) * SUB)

    for copy in small_copies:
        copy.wait()
    row_ids = lax.broadcasted_iota(jnp.int32, (SUB, SUB), 0)
    col_ids = lax.broadcasted_iota(jnp.int32, (SUB, SUB), 1)
    upper = jnp.where(row_ids <= col_ids, 1.0, 0.0).astype(jnp.float32)
    stacked_decay = jnp.concatenate([decay_ref[:, span_of(b)] for b in range(blocks)], axis=0)
    stacked_step = jnp.concatenate([step_ref[:, span_of(b)] for b in range(blocks)], axis=0)
    cum = (
        jnp.dot(stacked_decay, upper, precision=EXACT, preferred_element_type=jnp.float32)
        * LOG2E
    )
    feed = stacked_step * jnp.exp2(cum[:, SUB - 1 : SUB] - cum)
    grow = jnp.exp2(cum)
    shift[...] = cum - jnp.log2(stacked_step)

    def split(value):
        high = value.astype(jnp.bfloat16).astype(jnp.float32)
        return [high, value - high]

    slot_ids = lax.broadcasted_iota(jnp.int32, (LANES, depth), 0)
    head_ids = lax.broadcasted_iota(jnp.int32, (LANES, depth), 1) // head_width
    hit = slot_ids % heads == head_ids
    first = slot_ids // (2 * heads)
    pick_feed = jnp.where(jnp.logical_and(hit, first == 0), 1.0, 0.0).astype(jnp.bfloat16)
    pick_grow = jnp.where(jnp.logical_and(hit, first == 1), 1.0, 0.0).astype(jnp.bfloat16)
    filler = jnp.zeros((LANES - 5 * heads, SUB), jnp.float32)
    signal_copy.wait()
    for b in range(blocks):
        span = span_of(b)
        mine = slice(b * heads, (b + 1) * heads)
        cols = jnp.transpose(
            jnp.concatenate(split(feed[mine]) + split(grow[mine]) + [cum[mine], filler], axis=0)
        )
        cum_cols[b] = cols
        slim = cols.astype(jnp.bfloat16)
        wide_feed = jnp.dot(slim, pick_feed, preferred_element_type=jnp.float32)
        spread[span, :] = jnp.dot(slim, pick_grow, preferred_element_type=jnp.float32)
        feed_rows = (signal_ref[span, :].astype(jnp.float32) * wide_feed).astype(jnp.bfloat16)
        keys_t = jnp.transpose(keys_ref[span, :].astype(jnp.float32)).astype(jnp.bfloat16)
        local[b] = jnp.dot(keys_t, feed_rows, preferred_element_type=jnp.float32)

    def block_decay(b):
        last = (b + 1) * SUB - 1
        return spread[last : last + 1, :]

    def relay_copy(c):
        n = state_width // RELAY_CHUNKS
        part = pl.ds(c * n, n)
        return remote(
            relay_out.at[part],
            relay_in.at[part],
            relay_send.at[c],
            relay_recv.at[c],
            {"seq": (seq + 1) % seq_count},
        )

    @pl.when(seq == 0)
    def _():
        relay_in[...] = jnp.zeros_like(relay_in)

    def relay():
        for c in range(RELAY_CHUNKS):
            n = state_width // RELAY_CHUNKS
            part = slice(c * n, (c + 1) * n)

            @pl.when(seq > 0)
            def _():
                relay_copy(c).wait_recv()

            @pl.when(seq < seq_count - 1)
            def _():
                state = relay_in[part, :].astype(jnp.float32)
                for b in range(blocks):
                    state = block_decay(b) * state + local[b, part, :]
                relay_out[part, :] = state.astype(jnp.bfloat16)
                relay_copy(c).start()

    low_lane = lax.broadcasted_iota(jnp.int32, (SUB, LANES), 1) < head_width
    low_row = lax.broadcasted_iota(jnp.int32, (1, LANES), 1) < head_width
    none = jnp.zeros((SUB, LANES), jnp.bfloat16)

    def inner_block(b):
        span = span_of(b)
        scores = lax.dot_general(
            query_ref[span, :],
            keys_ref[span, :],
            (((1,), (1,)), ((), ())),
            preferred_element_type=jnp.float32,
        )
        scores = jnp.where(row_ids >= col_ids, scores, 0.0)
        for p in range(pair_count):
            cols = slice(p * LANES, (p + 1) * LANES)
            weights = []
            for h in (2 * p, 2 * p + 1):
                at = 4 * heads + h
                gaps = cum_cols[b, :, at : at + 1] - shift[b * heads + h : b * heads + h + 1, :]
                weights.append(
                    (scores * jnp.exp2(jnp.minimum(gaps, 100.0))).astype(jnp.bfloat16)
                )
            pair = signal_ref[span, cols]
            apart = jnp.concatenate(
                [jnp.where(low_lane, pair, none), jnp.where(low_lane, none, pair)], axis=0
            )
            skip = jnp.where(low_row, skip_ref[2 * p], skip_ref[2 * p + 1])
            inner[span, cols] = jnp.dot(
                jnp.concatenate(weights, axis=1), apart, preferred_element_type=jnp.float32
            ) + skip * pair.astype(jnp.float32)

    def gate_block(b, state):
        span = span_of(b)
        carried = state.astype(jnp.bfloat16)
        squared = jnp.zeros((SUB, LANES), jnp.float32)
        for p in range(depth // TILE):
            wide = slice(p * TILE, (p + 1) * TILE)
            read = jnp.dot(query_ref[span, :], carried[:, wide], preferred_element_type=jnp.float32)
            gate = gate_ref[span, wide].astype(jnp.float32)
            half = 0.5 * gate
            gated = (inner[span, wide] + spread[span, wide] * read) * (half + half * jnp.tanh(half))
            both = gated * gated
            squared = squared + both[:, :LANES] + both[:, LANES:]
            gained[span, wide] = (gated * gain_ref[:, wide]).astype(jnp.bfloat16)
        square_row[:, span] = jnp.sum(jnp.transpose(squared), axis=0, keepdims=True)

    def a_copy(u):
        at = pl.ds(*units[u])
        return remote(
            gained.at[at, pl.ds(0, depth)],
            gained.at[at, pl.ds(depth, depth)],
            a_send.at[0],
            a_recv.at[u],
            y_peer,
        )

    def sq_copy(d):
        return remote(
            square_row,
            sq_in.at[me],
            sq_send.at[d],
            sq_recv.at[me],
            {"mp": (me + d) % count},
        )

    def sq_arrival(source):
        return remote(square_row, sq_in.at[source], sq_send.at[0], sq_recv.at[source], y_peer)

    def z_copy(j, z, unit, at, size, way):
        recv = low_recv if way > 0 else high_recv
        dest = from_low if way > 0 else from_high
        rows, cols = pl.ds(at, size), cols_of(j)
        return remote(
            own.at[j // parts, rows, cols],
            dest.at[z, rows, cols],
            z_send.at[0],
            recv.at[z, j % parts, unit],
            {"mp": (zm + way) * PAIRS + ym},
        )

    def z_arrival(j, z, unit, at, size, way):
        recv = low_recv if way > 0 else high_recv
        dest = from_low if way > 0 else from_high
        piece = dest.at[z, pl.ds(at, size), cols_of(j)]
        return remote(
            piece, piece, z_send.at[0], recv.at[z, j % parts, unit], {"mp": (zm - way) * PAIRS + ym}
        )

    def multiply(j, at, size):
        total[pl.ds(0, size), :] = jnp.dot(
            gained[pl.ds(at, size), :],
            wbuf[j // parts, :, cols_of(j)],
            preferred_element_type=jnp.float32,
        )

    def gather(j, z, unit, at, size, base):
        rows = pl.ds(base, size)

        @pl.when(jnp.logical_and(z >= zm, zm > 0))
        def _():
            z_arrival(j, z, unit, at, size, 1).wait_recv()
            total[rows, :] += from_low[z, pl.ds(at, size), cols_of(j)].astype(jnp.float32)

        @pl.when(jnp.logical_and(z <= zm, zm < lines - 1))
        def _():
            z_arrival(j, z, unit, at, size, -1).wait_recv()
            total[rows, :] += from_high[z, pl.ds(at, size), cols_of(j)].astype(jnp.float32)

        return rows

    def pass_on(j, unit, at, size, base):
        z = target_of(j // parts)
        rows = gather(j, z, unit, at, size, base)
        own[j // parts, pl.ds(at, size), cols_of(j)] = total[rows, :].astype(jnp.bfloat16)

        @pl.when(z > zm)
        def _():
            z_copy(j, z, unit, at, size, 1).start()

        @pl.when(z < zm)
        def _():
            z_copy(j, z, unit, at, size, -1).start()

    def wide_step(j, lo, hi):
        start = units[lo][0]
        multiply(j, start, units[hi - 1][0] + units[hi - 1][1] - start)
        for u in range(lo, hi):
            at, size = units[u]
            pass_on(j, u, at, size, at - start)

    lower = zm < lines // 2
    at_end = zm * (lines - 1 - zm) == 0
    inside = zm * (lines - 1 - zm) > 0

    def hop_copy(h, src, dst, recv, device):
        cols = cols_of(h)
        return remote(src.at[:, cols], dst.at[:, cols], cross_send.at[0], recv.at[h], device)

    def line_device(way):
        return {"mp": (zm + way) * PAIRS + ym}

    def first_step(h):
        cols = cols_of(h)
        top = pl.ds(0, SUB)
        own_heads = gained[top, pl.ds(0, depth)]
        total[top, :] = jnp.dot(
            own_heads, wbuf[0, pl.ds(0, depth), cols], preferred_element_type=jnp.float32
        )
        pass_on(h, 0, 0, SUB, 0)
        total[top, :] = jnp.dot(own_heads, w_cross[:, cols], preferred_element_type=jnp.float32)

        @pl.when(jnp.logical_and(lower, zm > 0))
        def _():
            hop_copy(h, up_in, up_in, up_recv, y_peer).wait_recv()
            total[top, :] += up_in[:, cols].astype(jnp.float32)

        @pl.when(jnp.logical_and(zm >= lines // 2, zm < lines - 1))
        def _():
            hop_copy(h, down_in, down_in, down_recv, y_peer).wait_recv()
            total[top, :] += down_in[:, cols].astype(jnp.float32)

        cross_out[:, cols] = total[top, :].astype(jnp.bfloat16)

        @pl.when(lower)
        def _():
            hop_copy(h, cross_out, up_in, up_recv, line_device(1)).start()

        @pl.when(zm >= lines // 2)
        def _():
            hop_copy(h, cross_out, down_in, down_recv, line_device(-1)).start()

    def hand_on(h, last):
        @pl.when(lower)
        def _():
            hop_copy(h, down_in, down_in, down_recv, y_peer).wait_recv()
            if last:
                hop_copy(h, down_in, last_in, last_recv, y_peer).start()
            else:
                hop_copy(h, down_in, down_in, down_recv, line_device(-1)).start()

        @pl.when(zm >= lines // 2)
        def _():
            hop_copy(h, up_in, up_in, up_recv, y_peer).wait_recv()
            if last:
                hop_copy(h, up_in, last_in, last_recv, y_peer).start()
            else:
                hop_copy(h, up_in, up_in, up_recv, line_device(1)).start()

    def first_steps(lo, hi):
        @pl.loop(lo, hi)
        def _(h):
            first_step(h)

    pl.when(seq == 0)(relay)
    inner_block(0)
    pl.when(seq == 1)(relay)
    inner_block(1)
    inner_block(2)
    pl.when(seq == 2)(relay)
    for b in range(3, blocks):
        inner_block(b)
    from_y(0)
    from_y(1)
    pl.when(seq >= 3)(relay)

    gate_copy.wait()
    w_copy(0).wait()
    w_cross_copy().wait()
    early = parts // 2
    ready = parts + early
    last_unit = len(units)
    fine_end = last_unit - tokens // 2 // SUB

    state = relay_in[...].astype(jnp.float32)
    for b in range(blocks):
        gate_block(b, state)
        if b < blocks - 1:
            state = block_decay(b) * state + local[b]
        if b == 0:
            pl.when(at_end)(lambda: first_steps(0, early))
        if b == 1:
            for u in range(1, fine_end):
                a_copy(u).start()
            pl.when(at_end)(lambda: first_steps(early, parts))
            if parts > 2:
                from_y(2)
            from_x(0)
        if b == 2:
            a_copy(fine_end).start()
            for j in range(parts, ready):
                wy_copy(j).start()
            a_copy(0).start()
            for j in range(3, parts):
                from_y(j)
            from_x(1)
    for u in range(fine_end + 1, last_unit):
        a_copy(u).start()
    for j in range(ready, 2 * parts):
        wy_copy(j).start()
    for d in range(1, count):
        sq_copy(d).start()
    for t in range(1, lines):
        w_copy(t).wait()
    for j in range(2, parts - 1):
        from_x(j)
    pl.when(inside)(lambda: first_steps(0, parts))

    for u in range(1, fine_end + 1):
        a_copy(u).wait_recv()

        @pl.loop(0, parts)
        def _(j):
            if u == 1:
                if parts > 2:
                    pl.when(j == parts - 1)(lambda: from_x(parts - 1))
                ensure(j)
            if u == fine_end:
                pl.when(j == parts - 2)(lambda: from_y_next(parts))

                @pl.when(j == parts - 1)
                def _():
                    for k in range(parts + 1, ready):
                        from_y_next(k)

            wide_step(j, u, u + 1)

    from_x(parts)
    for j in range(parts, ready):
        ensure(j)
        wide_step(j, 1, fine_end + 1)
        if j + 1 < ready:
            from_x(j + 1)

    a_copy(0).wait_recv()

    @pl.loop(parts, ready)
    def _(j):
        wide_step(j, 0, 1)

    @pl.when(inside)
    def _():
        for h in range(parts):
            hand_on(h, False)

    for u in range(fine_end + 1, last_unit):
        a_copy(u).wait_recv()
    marks = [(2, ready), (4, ready + 1)]

    @pl.loop(0, ready)
    def _(k):
        for at, j in marks:
            if at < ready:
                pl.when(k == at)(lambda: from_y_next(j))
        wide_step(k, fine_end + 1, last_unit)

    for at, j in marks:
        if at >= ready:
            from_y_next(j)
    from_x(ready)
    from_y_next(ready + 2)
    ensure(ready)
    wide_step(ready, 0, fine_end)
    from_x(ready + 1)
    from_y_next(ready + 3)
    wide_step(ready, fine_end, last_unit)

    squares = square_row[...]
    for d in range(1, count):
        source = (me + d) % count
        sq_arrival(source).wait_recv()
        squares = squares + sq_in[source]
    inverse = 1.0 / jnp.sqrt(squares / (count * depth) + 1e-05)
    scaling = jnp.transpose(jnp.broadcast_to(inverse, (LANES, tokens)))
    spread[:, pl.ds(0, LANES)] = scaling

    def out_copy(j, u):
        rows, cols = pl.ds(*units[u]), cols_of(j)
        return pltpu.make_async_copy(
            out_ref.at[rows, cols], out_hbm.at[rows, cols], out_sem.at[j % parts, u]
        )

    def ahead(j):
        pl.when(j == ready + 2)(lambda: from_y_next(j + 2))
        pl.when(j + 1 < chunks)(lambda: from_x(j + 1))
        pl.when(jnp.logical_and(j > ready + 1, j + 3 < chunks))(lambda: from_y_next(j + 3))
        ensure(j)

    @pl.loop(ready + 1, (lines - 1) * parts)
    def _(j):
        @pl.when(jnp.logical_and(at_end, j == (lines - 1) * parts - 2))
        def _():
            for h in range(parts):
                hand_on(h, True)

        ahead(j)
        wide_step(j, 0, last_unit)

    @pl.loop((lines - 1) * parts, chunks)
    def _(j):
        ahead(j)
        multiply(j, 0, tokens)
        for u, (at, size) in enumerate(units):
            gather(j, zm, u, at, size, at)
            if u == 0:

                @pl.when(at_end)
                def _():
                    h = j % parts
                    hop_copy(h, last_in, last_in, last_recv, y_peer).wait_recv()
                    total[:size, :] += last_in[:, cols_of(h)].astype(jnp.float32)

            factor = spread[at : at + size, :LANES]
            for k in range(TILE // LANES):
                cols = pl.ds(pl.multiple_of((j % parts) * TILE + k * LANES, LANES), LANES)
                out_ref[pl.ds(at, size), cols] = (
                    total[at : at + size, k * LANES : (k + 1) * LANES] * factor
                ).astype(jnp.bfloat16)
            out_copy(j, u).start()

    for j in range(parts):
        for u in range(last_unit):
            out_copy(j, u).wait()
    sends = wbuf.at[:, pl.ds(0, quarter)]
    for sem in (wy_send, wx_send, wc_send, wd_send):
        remote(sends, sends, sem.at[0], wy_recv.at[0], y_peer).wait_send()
    sends = gained.at[:, pl.ds(0, depth)]
    remote(sends, sends, a_send.at[0], a_recv.at[0], y_peer).wait_send()
    remote(own, own, z_send.at[0], a_recv.at[0], y_peer).wait_send()
    sends = own.at[0, pl.ds(0, 2 * SUB)]
    remote(sends, sends, cross_send.at[0], a_recv.at[0], y_peer).wait_send()
    for d in range(1, count):
        sq_copy(d).wait_send()

    @pl.when(seq < seq_count - 1)
    def _():
        for c in range(RELAY_CHUNKS):
            relay_copy(c).wait_send()


def on_device(
    signal,
    gate_input,
    input_map,
    output_map,
    log_decay,
    step_size,
    skip_gain,
    norm_gain,
    out_weight,
):
    tokens, depth = signal.shape
    heads = skip_gain.shape[0]
    state_width = input_map.shape[1]
    count = lax.axis_size("mp")
    lines = count // PAIRS
    width = out_weight.shape[1] // count
    parts = width // TILE
    chunks = lines * parts
    blocks = tokens // SUB
    units = len(units_of(tokens))
    dma = pltpu.SemaphoreType.DMA
    held = lambda n: pltpu.VMEM((n, tokens, width), jnp.bfloat16)
    anywhere = pl.BlockSpec(memory_space=pl.ANY)
    return pl.pallas_call(
        layer_kernel,
        out_shape=jax.ShapeDtypeStruct((tokens, width), jnp.bfloat16),
        in_specs=[anywhere] * 6
        + [pl.BlockSpec(memory_space=pltpu.SMEM)]
        + [anywhere] * 2,
        out_specs=anywhere,
        scratch_shapes=[
            pltpu.VMEM((tokens, width), jnp.bfloat16),
            pltpu.VMEM((tokens, depth), jnp.bfloat16),
            pltpu.VMEM((tokens, depth), jnp.bfloat16),
            pltpu.VMEM((tokens, state_width), jnp.bfloat16),
            pltpu.VMEM((tokens, state_width), jnp.bfloat16),
            pltpu.VMEM((heads, tokens), jnp.float32),
            pltpu.VMEM((heads, tokens), jnp.float32),
            pltpu.VMEM((1, depth), jnp.float32),
            pltpu.VMEM((tokens, 2 * depth), jnp.bfloat16),
            pltpu.VMEM((1, tokens), jnp.float32),
            pltpu.VMEM((tokens, depth), jnp.float32),
            pltpu.VMEM((blocks, state_width, depth), jnp.float32),
            pltpu.VMEM((tokens, depth), jnp.float32),
            pltpu.VMEM((blocks * heads, SUB), jnp.float32),
            pltpu.VMEM((blocks, SUB, LANES), jnp.float32),
            pltpu.VMEM((state_width, depth), jnp.bfloat16),
            pltpu.VMEM((state_width, depth), jnp.bfloat16),
            pltpu.VMEM((lines, 2 * depth, width), jnp.bfloat16),
            held(lines - 1),
            held(lines),
            held(lines),
            pltpu.VMEM((tokens, TILE), jnp.float32),
            pltpu.VMEM((depth, width), jnp.bfloat16),
            pltpu.VMEM((SUB, width), jnp.bfloat16),
            pltpu.VMEM((SUB, width), jnp.bfloat16),
            pltpu.VMEM((SUB, width), jnp.bfloat16),
            pltpu.VMEM((SUB, width), jnp.bfloat16),
            pltpu.VMEM((count, 1, tokens), jnp.float32),
            dma((7,)),
            dma((parts, units)),
            dma((lines + 1,)),
            dma((1,)),
            dma((chunks,)),
            dma((1,)),
            dma((chunks,)),
            dma((1,)),
            dma((chunks,)),
            dma((1,)),
            dma((chunks,)),
            dma((1,)),
            dma((units,)),
            dma((1,)),
            dma((lines, parts, units)),
            dma((lines, parts, units)),
            dma((1,)),
            dma((parts,)),
            dma((parts,)),
            dma((parts,)),
            dma((count,)),
            dma((count,)),
            dma((RELAY_CHUNKS,)),
            dma((RELAY_CHUNKS,)),
        ],
        compiler_params=pltpu.CompilerParams(
            collective_id=0, has_side_effects=True, vmem_limit_bytes=58 << 20
        ),
        name="layer",
    )(
        signal,
        gate_input,
        input_map,
        output_map,
        jnp.transpose(log_decay),
        jnp.transpose(step_size),
        skip_gain,
        norm_gain[None],
        out_weight,
    )


def solution(mesh):
    placed = (
        P("seq", "mp"),
        P("seq", "mp"),
        P("seq", None),
        P("seq", None),
        P("seq", "mp"),
        P("seq", "mp"),
        P("mp"),
        P("mp"),
        P("mp", None),
    )
    return jax.shard_map(
        on_device, mesh=mesh, in_specs=placed, out_specs=P("seq", "mp"), check_vma=False
    )
```
